32 devices in a mesh: seq: 8 (over z, x), head: 4 (over y, core).
Axes of the slice: x: 2, y: 2, z: 4, core: 2. Of those that a mesh axis runs over, the one named last changes fastest.
Arguments:
- context: bfloat16 [16384, 2048], P('seq'), may hold values from -64 to 64
- wq_cross: bfloat16 [2048, 2048], P(None, 'head'), may hold values from -4 to 4
- wk_cross: bfloat16 [2048, 2048], P(None, 'head'), may hold values from -4 to 4
- wv_cross: bfloat16 [2048, 2048], P(None, 'head'), may hold values from -0.125 to 0.125
- wo_cross: bfloat16 [2048, 2048], P('head'), may hold values from -0.125 to 0.125
- wq_latent: bfloat16 [2048, 2048], P(None, 'head'), may hold values from -4 to 4
- wk_latent: bfloat16 [2048, 2048], P(None, 'head'), may hold values from -4 to 4
- wv_latent: bfloat16 [2048, 2048], P(None, 'head'), may hold values from -0.125 to 0.125
- wo_latent: bfloat16 [2048, 2048], P('head'), may hold values from -0.125 to 0.125
- cross_keep: int32 [16, 2048, 2048], P('head', None, 'seq'), may hold values from 0 to 255, as said below
- latent_keep: int32 [16, 2048, 128], P('head'), may hold values from 0 to 65535, as said below
- residual_keep: int32 [2, 2048, 128], replicated, may hold values from 0 to 65535, as said below
Outputs:
- latents_out: bfloat16 [2048, 2048], P('seq', 'head')
The draws below stay inside these ranges and needn't reach their ends.
Inputs may be any that keep to these rules, and one draw needn't show every extreme that they name: `cross_keep`: each of the 8 low bits of a word is one keep flag, laid out as the steps say. `latent_keep`: each of the 16 low bits of a word is one keep flag, laid out as the steps say. `residual_keep`: each of the 16 low bits of a word is one keep flag, laid out as the steps say.
All inputs are finite; a program needn't handle non-finite values.
Results may differ from the reference program's by a relative error of at most 0.015.
Values may be sent and summed in bfloat16 or wider, within the bound.
A program may use at most 128 MiB of HBM per device.

```python
import math
import jax
import jax.numpy as jnp
from jax import lax

D = 2048
HEADS = 16
HEAD_DIM = 128
NL = 2048
TOKENS = 16384
N_SEQ = 8


def draw_context(key, part):
    columns = jnp.arange(D, dtype=jnp.float32) / max(D - 1, 1)
    row_scale = jnp.exp(jax.random.uniform(jax.random.fold_in(key, 301), (TOKENS, 1), jnp.float32, jnp.log(0.3), jnp.log(3.0)))
    base_draw = jnp.clip(jax.random.normal(jax.random.fold_in(key, 303), (TOKENS, D), jnp.float32), -4.5, 4.5)
    column_ramp = 10.0 ** (columns - 0.5)
    return (base_draw * column_ramp[None, :] * row_scale).astype(jnp.bfloat16)


def score_weight(key, pair_index, side_index):
    model_width = HEADS * HEAD_DIM
    own_part = jnp.clip(jax.random.normal(jax.random.fold_in(key, 400 + 10 * pair_index + side_index), (D, model_width), jnp.float32), -4.5, 4.5)
    entries = 1.7 * own_part
    return (entries / jnp.sqrt(D * 1.0)).astype(jnp.bfloat16)


def draw_wq_cross(key, part):
    return score_weight(key, 0, 0)


def draw_wk_cross(key, part):
    return score_weight(key, 0, 1)


def draw_wq_latent(key, part):
    return score_weight(key, 1, 0)


def draw_wk_latent(key, part):
    return score_weight(key, 1, 1)


def keep_words(key, salt_value, shape, word_bits):
    highest = 2 ** word_bits
    first = jax.random.randint(jax.random.fold_in(key, salt_value), shape, 0, highest, dtype=jnp.int32)
    second = jax.random.randint(jax.random.fold_in(key, salt_value + 1), shape, 0, highest, dtype=jnp.int32)
    third = jax.random.randint(jax.random.fold_in(key, salt_value + 2), shape, 0, highest, dtype=jnp.int32)
    return first | second | third


def draw_cross_keep(key, part):
    return keep_words(key, 500, (HEADS, NL, TOKENS // 8), 8)


def draw_latent_keep(key, part):
    return keep_words(key, 600, (HEADS, NL, NL // 16), 16)


def draw_residual_keep(key, part):
    return keep_words(key, 700, (2, NL, D // 16), 16)


def steps_of(stream_key, extent, split, low, top_value):
    gain, own = 1.0, jax.random.fold_in(stream_key, 6)
    for position, blocks in split:
        draws = jnp.exp(jax.random.uniform(jax.random.fold_in(own, position), (blocks,), jnp.float32, low / len(split), top_value / len(split)))
        gain = gain * jnp.repeat(draws, extent[position] // blocks).reshape([-1 if axis == position else 1 for axis in range(len(extent))])
    return gain


def bell_draw(stream_key, shape, spread, reach, shards=(), kind=jnp.bfloat16):
    values = jax.random.normal(stream_key, shape, jnp.float32) * spread
    if len(shards) > 0:
        values = steps_of(stream_key, shape, shards, -0.22, 0.18) * values
    return jnp.clip(values, min=-reach, max=reach).astype(kind)


def setup_inputs(seed: int = 0) -> dict:
    splits = jax.random.split(jax.random.key(seed), 13)
    return {
        "context": draw_context(jax.random.fold_in(splits[12], 71), 0),
        "wq_cross": draw_wq_cross(jax.random.fold_in(splits[12], 71), 0),
        "wk_cross": draw_wk_cross(jax.random.fold_in(splits[12], 71), 0),
        "wv_cross": bell_draw(splits[3], (D, HEADS * HEAD_DIM), D ** -0.5, 0.125, ((1, 4),)),
        "wo_cross": bell_draw(splits[4], (HEADS * HEAD_DIM, D), (HEADS * HEAD_DIM) ** -0.5, 0.125, ((0, 4),)),
        "wq_latent": draw_wq_latent(jax.random.fold_in(splits[12], 71), 0),
        "wk_latent": draw_wk_latent(jax.random.fold_in(splits[12], 71), 0),
        "wv_latent": bell_draw(splits[7], (D, HEADS * HEAD_DIM), D ** -0.5, 0.125, ((1, 4),)),
        "wo_latent": bell_draw(splits[8], (HEADS * HEAD_DIM, D), (HEADS * HEAD_DIM) ** -0.5, 0.125, ((0, 4),)),
        "cross_keep": draw_cross_keep(jax.random.fold_in(splits[12], 71), 0),
        "latent_keep": draw_latent_keep(jax.random.fold_in(splits[12], 71), 0),
        "residual_keep": draw_residual_keep(jax.random.fold_in(splits[12], 71), 0),
    }


keep_scale = 8.0 / 7.0

def unpack_bits(packed_words, word_bits):
    shifts = jnp.arange(word_bits, dtype=jnp.int32)
    bit_table = jnp.bitwise_and(jnp.right_shift(packed_words[..., None, :], shifts[:, None]), 1)
    return bit_table.reshape(packed_words.shape[:-1] + (word_bits * packed_words.shape[-1],))

def rms_rows(matrix):
    wide_rows = matrix.astype(jnp.float32)
    mean_square = lax.optimization_barrier(jnp.mean(wide_rows * wide_rows, axis=-1, keepdims=True))
    return (wide_rows * lax.rsqrt(mean_square + 1e-06)).astype(jnp.bfloat16)

def split_heads(matrix):
    return matrix.reshape(matrix.shape[0], HEADS, HEAD_DIM).transpose(1, 0, 2)

def join_heads(stacked):
    return stacked.transpose(1, 0, 2).reshape(stacked.shape[1], HEADS * HEAD_DIM).astype(jnp.bfloat16)

def attend(queries, key_rows, value_rows, packed, groups, word_bits, query_pos, key_pos):
    score_scale = 1.0 / math.sqrt(HEAD_DIM)

    def one_head(head_items):
        query_rows, head_keys, head_values, packed_words = head_items
        scores = jnp.dot(query_rows, head_keys.T, preferred_element_type=jnp.float32) * score_scale
        allowed = key_pos[None, :] <= query_pos[:, None]
        scores = jnp.where(allowed, scores, -1e+30)
        row_top = lax.optimization_barrier(jnp.max(scores, axis=-1, keepdims=True))
        exponent = jnp.where(allowed, jnp.exp(scores - row_top), 0.0)
        row_sum = lax.optimization_barrier(jnp.sum(exponent, axis=-1, keepdims=True))
        grouped = packed_words.reshape(packed_words.shape[0], groups, -1)
        keep_flags = unpack_bits(grouped, word_bits).reshape(packed_words.shape[0], -1).astype(jnp.float32)
        weights = (exponent / row_sum * keep_flags * keep_scale).astype(jnp.bfloat16)
        return jnp.dot(weights, head_values, preferred_element_type=jnp.float32)
    return lax.map(one_head, (queries, key_rows, value_rows, packed))

def reference(context, wq_cross, wk_cross, wv_cross, wo_cross, wq_latent, wk_latent, wv_latent, wo_latent, cross_keep, latent_keep, residual_keep):
    first_latent = TOKENS - NL
    normed = rms_rows(context)
    key_rows = jnp.dot(normed, wk_cross, preferred_element_type=jnp.float32).astype(jnp.bfloat16)
    value_rows = jnp.dot(normed, wv_cross, preferred_element_type=jnp.float32).astype(jnp.bfloat16)
    queries = jnp.dot(normed[first_latent:], wq_cross, preferred_element_type=jnp.float32).astype(jnp.bfloat16)
    latent_pos = jnp.arange(NL, dtype=jnp.int32)
    context_pos = jnp.arange(TOKENS, dtype=jnp.int32)
    attended = join_heads(attend(split_heads(queries), split_heads(key_rows), split_heads(value_rows), cross_keep, N_SEQ, 8, first_latent + latent_pos, context_pos))
    residual_flags = unpack_bits(residual_keep, 16).astype(jnp.float32)
    branch = jnp.dot(attended, wo_cross, preferred_element_type=jnp.float32)
    latents = (context[first_latent:].astype(jnp.float32) + residual_flags[0] * keep_scale * branch).astype(jnp.bfloat16)
    normed_latents = rms_rows(latents)
    latent_queries = jnp.dot(normed_latents, wq_latent, preferred_element_type=jnp.float32).astype(jnp.bfloat16)
    latent_keys = jnp.dot(normed_latents, wk_latent, preferred_element_type=jnp.float32).astype(jnp.bfloat16)
    latent_values = jnp.dot(normed_latents, wv_latent, preferred_element_type=jnp.float32).astype(jnp.bfloat16)
    latent_attended = join_heads(attend(split_heads(latent_queries), split_heads(latent_keys), split_heads(latent_values), latent_keep, 1, 16, latent_pos, latent_pos))
    latent_branch = jnp.dot(latent_attended, wo_latent, preferred_element_type=jnp.float32)
    return (latents.astype(jnp.float32) + residual_flags[1] * keep_scale * latent_branch).astype(jnp.bfloat16)
```

```python
import functools
import math

import jax
import jax.numpy as jnp
from jax import lax
from jax.experimental import pallas as pl
from jax.experimental.pallas import tpu as pltpu
from jax.sharding import PartitionSpec as P

keep_scale = 8.0 / 7.0
masked = -1e30
log2e = 1.4426950408889634
MESH = pl.DeviceIdType.MESH
ANY = pl.BlockSpec(memory_space=pl.ANY)


def unpack_bits(packed_words, word_bits):
    shifts = jnp.arange(word_bits, dtype=jnp.int32)
    bit_table = jnp.bitwise_and(jnp.right_shift(packed_words[..., None, :], shifts[:, None]), 1)
    return bit_table.reshape(packed_words.shape[:-1] + (word_bits * packed_words.shape[-1],))


def rms_rows(matrix):
    wide_rows = matrix.astype(jnp.float32)
    mean_square = jnp.mean(wide_rows * wide_rows, axis=-1, keepdims=True)
    return (wide_rows * lax.rsqrt(mean_square + 1e-06)).astype(jnp.bfloat16)


def greet(axis, n, me):
    barrier = pltpu.get_barrier_semaphore()
    for d in range(1, n):
        pl.semaphore_signal(
            barrier, inc=1, device_id={axis: lax.rem(me + d, n)}, device_id_type=MESH
        )
    pl.semaphore_wait(barrier, n - 1)


def exchange_kernel(axis, n, modes, widths, *refs):
    count = len(modes)
    ins, outs = refs[:count], refs[count : 2 * count]
    send_sem, recv_sem, local_sem = refs[2 * count :]
    me = lax.axis_index(axis)

    def piece(a, j):
        if modes[a] == "lead":
            return ins[a].at[j]
        if modes[a] == "cols":
            start = pl.multiple_of(j * widths[a], 128)
            return ins[a].at[:, pl.ds(start, widths[a])]
        return ins[a]

    local = []
    for a in range(count):
        copy = pltpu.make_async_copy(piece(a, me), outs[a].at[me], local_sem.at[a])
        copy.start()
        local.append(copy)
    greet(axis, n, me)
    copies = []
    for d in range(1, n):
        to = lax.rem(me + d, n)
        for a in range(count):
            copy = pltpu.make_async_remote_copy(
                src_ref=piece(a, to),
                dst_ref=outs[a].at[me],
                send_sem=send_sem.at[a, d],
                recv_sem=recv_sem.at[a, d],
                device_id={axis: to},
                device_id_type=MESH,
            )
            copy.start()
            copies.append(copy)
    for copy in copies:
        copy.wait()
    for copy in local:
        copy.wait()


def exchange(arrays, modes, axis, ident):
    n = lax.axis_size(axis)
    shapes, widths = [], []
    for x, mode in zip(arrays, modes):
        if mode == "lead":
            shape, width = x.shape, 0
        elif mode == "cols":
            width = x.shape[1] // n
            shape = (n, x.shape[0], width)
        else:
            shape, width = (n,) + x.shape, 0
        shapes.append(jax.ShapeDtypeStruct(shape, x.dtype))
        widths.append(width)
    return pl.pallas_call(
        functools.partial(exchange_kernel, axis, n, tuple(modes), tuple(widths)),
        out_shape=tuple(shapes),
        in_specs=[ANY] * len(arrays),
        out_specs=tuple([ANY] * len(arrays)),
        scratch_shapes=[
            pltpu.SemaphoreType.DMA((len(arrays), n)),
            pltpu.SemaphoreType.DMA((len(arrays), n)),
            pltpu.SemaphoreType.DMA((len(arrays),)),
        ],
        compiler_params=pltpu.CompilerParams(collective_id=ident, has_side_effects=True),
    )(*arrays)


def spread_kernel(axis, n, x_ref, out_ref, send_a, recv_a, send_b, recv_b, local_sem):
    me = lax.axis_index(axis)
    root = n - 1
    greet(axis, n, me)

    def parts(j):
        return (pl.ds(j * n, n), pl.ds(root * n + j, 1))

    tail = pl.ds(root * n + root, 1)

    def remote(src, dst, send, recv, to):
        return pltpu.make_async_remote_copy(
            src_ref=src,
            dst_ref=dst,
            send_sem=send,
            recv_sem=recv,
            device_id={axis: to},
            device_id_type=MESH,
        )

    @pl.when(me == root)
    def _():
        copies = []
        for j in range(root):
            for p, part in enumerate(parts(j)):
                copies.append(
                    remote(x_ref.at[part], out_ref.at[part], send_a.at[p, j], recv_a.at[p], j)
                )
                copies[-1].start()
        for j in range(root):
            copies.append(
                remote(x_ref.at[tail], out_ref.at[tail], send_a.at[2, j], recv_a.at[2], j)
            )
            copies[-1].start()
        own = pltpu.make_async_copy(x_ref, out_ref, local_sem)
        own.start()
        for copy in copies:
            copy.wait_send()
        own.wait()

    @pl.when(me != root)
    def _():
        copies = []
        for p, part in enumerate(parts(me)):
            remote(x_ref.at[part], out_ref.at[part], send_a.at[p, 0], recv_a.at[p], root).wait_recv()
            for d in range(1, root):
                to = lax.rem(me + d, root)
                copies.append(
                    remote(
                        out_ref.at[part], out_ref.at[part], send_b.at[p, d], recv_b.at[p, d], to
                    )
                )
                copies[-1].start()
        remote(x_ref.at[tail], out_ref.at[tail], send_a.at[2, 0], recv_a.at[2], root).wait_recv()
        for copy in copies:
            copy.wait()


def spread(x, axis, ident):
    n = lax.axis_size(axis)
    rows, width = x.shape
    grains = x.reshape(n * n, rows // (n * n), width)
    out = pl.pallas_call(
        functools.partial(spread_kernel, axis, n),
        out_shape=jax.ShapeDtypeStruct(grains.shape, x.dtype),
        in_specs=[ANY],
        out_specs=ANY,
        scratch_shapes=[
            pltpu.SemaphoreType.DMA((3, n)),
            pltpu.SemaphoreType.DMA((3,)),
            pltpu.SemaphoreType.DMA((2, n)),
            pltpu.SemaphoreType.DMA((2, n)),
            pltpu.SemaphoreType.DMA,
        ],
        compiler_params=pltpu.CompilerParams(collective_id=ident, has_side_effects=True),
    )(grains)
    return out.reshape(rows, width)


def dot_t(a, b):
    return lax.dot_general(a, b, (((1,), (1,)), ((), ())), preferred_element_type=jnp.float32)


def fold_lanes(x, op):
    parts = [x[:, j : j + 128] for j in range(0, x.shape[1], 128)]
    return functools.reduce(op, parts)


def cross_kernel(n, hd, scale, q_ref, k_ref, v_ref, w_ref, o_ref, st_ref, s_ref):
    block, head = pl.program_id(0), pl.program_id(1)
    bq = q_ref.shape[0]
    keys = k_ref.shape[0]
    chunk = w_ref.shape[2]
    chunks = keys // chunk
    root = lax.axis_index("seq") == n - 1
    cols = pl.ds(pl.multiple_of(head * hd, 128), hd)
    factor = scale * log2e

    def finish(acc, top, total):
        o_ref[...] = (acc * (keep_scale / total)).astype(o_ref.dtype)
        stat = top * scale + jnp.log(total)
        lane = lax.broadcasted_iota(jnp.int32, st_ref.shape, 1)
        st_ref[...] = jnp.where(lane == head, stat, st_ref[...])

    @pl.when(head == 0)
    def _():
        st_ref[...] = jnp.zeros_like(st_ref)

    @pl.when(jnp.logical_not(root))
    def _():
        q = q_ref[...]
        tops = None
        for c in range(chunks):
            s = dot_t(q, k_ref[c * chunk : (c + 1) * chunk, cols])
            s_ref[c] = s
            t = fold_lanes(s, jnp.maximum)
            tops = t if tops is None else jnp.maximum(tops, t)
        top = jnp.max(tops, axis=1, keepdims=True)
        words = w_ref[0]
        acc = jnp.zeros((bq, hd), jnp.float32)
        sums = jnp.zeros((bq, 128), jnp.float32)
        for c in range(chunks):
            e = jnp.exp2((s_ref[c] - top) * factor)
            sums = sums + fold_lanes(e, jnp.add)
            weights = jnp.where((words & (1 << c)) != 0, e, 0.0).astype(jnp.bfloat16)
            acc = acc + jnp.dot(
                weights,
                v_ref[c * chunk : (c + 1) * chunk, cols],
                preferred_element_type=jnp.float32,
            )
        finish(acc, top, jnp.sum(sums, axis=1, keepdims=True))

    @pl.when(root)
    def _():
        q = q_ref[...]
        used = jnp.minimum(((block + 1) * bq + chunk - 1) // chunk, chunks)
        row = block * bq + lax.broadcasted_iota(jnp.int32, (bq, chunk), 0)
        lane = lax.broadcasted_iota(jnp.int32, (bq, chunk), 1)

        def first(c, tops):
            at = pl.ds(pl.multiple_of(c * chunk, chunk), chunk)
            s = dot_t(q, k_ref[at, cols])
            s = jnp.where(lane + c * chunk <= row, s, masked)
            s_ref[c] = s
            return jnp.maximum(tops, fold_lanes(s, jnp.maximum))

        tops = lax.fori_loop(0, used, first, jnp.full((bq, 128), masked, jnp.float32))
        top = jnp.max(tops, axis=1, keepdims=True)
        words = w_ref[0]

        def second(c, carry):
            acc, sums = carry
            at = pl.ds(pl.multiple_of(c * chunk, chunk), chunk)
            e = jnp.exp2((s_ref[c] - top) * factor)
            e = jnp.where(lane + c * chunk <= row, e, 0.0)
            sums = sums + fold_lanes(e, jnp.add)
            weights = jnp.where((words & (1 << c)) != 0, e, 0.0).astype(jnp.bfloat16)
            acc = acc + jnp.dot(weights, v_ref[at, cols], preferred_element_type=jnp.float32)
            return acc, sums

        acc, sums = lax.fori_loop(
            0,
            used,
            second,
            (jnp.zeros((bq, hd), jnp.float32), jnp.zeros((bq, 128), jnp.float32)),
        )
        finish(acc, top, jnp.sum(sums, axis=1, keepdims=True))


def cross_attention(queries, keys, values, words, n, hd):
    rows, width = queries.shape
    toks = keys.shape[0]
    heads = width // hd
    bq = min(256, rows)
    chunk = words.shape[2]
    return pl.pallas_call(
        functools.partial(cross_kernel, n, hd, 1.0 / math.sqrt(hd)),
        grid=(rows // bq, heads),
        in_specs=[
            pl.BlockSpec((bq, hd), lambda i, h: (i, h)),
            pl.BlockSpec((toks, width), lambda i, h: (0, 0)),
            pl.BlockSpec((toks, width), lambda i, h: (0, 0)),
            pl.BlockSpec((1, bq, chunk), lambda i, h: (h, i, 0)),
        ],
        out_specs=(
            pl.BlockSpec((bq, hd), lambda i, h: (i, h)),
            pl.BlockSpec((bq, 128), lambda i, h: (i, 0)),
        ),
        out_shape=(
            jax.ShapeDtypeStruct((rows, width), jnp.bfloat16),
            jax.ShapeDtypeStruct((rows, 128), jnp.float32),
        ),
        scratch_shapes=[pltpu.VMEM((toks // chunk, bq, chunk), jnp.float32)],
        cost_estimate=pl.CostEstimate(
            flops=4 * rows * toks * width * 4,
            transcendentals=heads * rows * toks,
            bytes_accessed=4 * heads * rows * chunk,
        ),
    )(queries, keys, values, words)


def latent_kernel(hd, scale, q_ref, k_ref, v_ref, w_ref, o_ref, s_ref):
    rows = q_ref.shape[0]
    pieces, piece_rows = k_ref.shape[0], k_ref.shape[1]
    chunk = w_ref.shape[2]
    factor = scale * log2e
    first_row = lax.axis_index("seq") * rows
    used = first_row + rows
    row = first_row + lax.broadcasted_iota(jnp.int32, (rows, chunk), 0)
    lane = lax.broadcasted_iota(jnp.int32, (rows, chunk), 1)
    per = piece_rows // chunk
    q = q_ref[...]
    words = w_ref[0]
    tops = jnp.full((rows, 128), masked, jnp.float32)
    for p in range(pieces):
        s = dot_t(q, k_ref[p])
        for j in range(per):
            c = p * per + j
            part = jnp.where(lane + c * chunk <= row, s[:, j * chunk : (j + 1) * chunk], masked)
            s_ref[c] = part
            tops = jnp.maximum(tops, part)
    top = jnp.max(tops, axis=1, keepdims=True)
    acc = jnp.zeros((rows, hd), jnp.float32)
    sums = jnp.zeros((rows, 128), jnp.float32)
    for p in range(pieces):
        kept = []
        for j in range(per):
            c = p * per + j
            e = jnp.exp2((s_ref[c] - top) * factor)
            e = jnp.where(lane + c * chunk <= row, e, 0.0)
            sums = sums + e
            kept.append(jnp.where((words & (1 << c)) != 0, e, 0.0).astype(jnp.bfloat16))
        weights = jnp.concatenate(kept, axis=1) if per > 1 else kept[0]
        acc = acc + jnp.dot(weights, v_ref[p], preferred_element_type=jnp.float32)
    total = jnp.sum(sums, axis=1, keepdims=True)
    o_ref[...] = (acc * (keep_scale / total)).astype(o_ref.dtype)


def latent_attention(queries, keys, values, words, hd):
    rows, width = queries.shape
    pieces, piece_rows, _ = keys.shape
    heads = width // hd
    chunk = words.shape[2]
    return pl.pallas_call(
        functools.partial(latent_kernel, hd, 1.0 / math.sqrt(hd)),
        grid=(heads,),
        in_specs=[
            pl.BlockSpec((rows, hd), lambda h: (0, h)),
            pl.BlockSpec((pieces, piece_rows, hd), lambda h: (0, 0, h)),
            pl.BlockSpec((pieces, piece_rows, hd), lambda h: (0, 0, h)),
            pl.BlockSpec((1, rows, chunk), lambda h: (h, 0, 0)),
        ],
        out_specs=pl.BlockSpec((rows, hd), lambda h: (0, h)),
        out_shape=jax.ShapeDtypeStruct((rows, width), jnp.bfloat16),
        scratch_shapes=[pltpu.VMEM((pieces * piece_rows // chunk, rows, chunk), jnp.float32)],
    )(queries, keys, values, words)


def per_device(
    context,
    wq_cross,
    wk_cross,
    wv_cross,
    wo_cross,
    wq_latent,
    wk_latent,
    wv_latent,
    wo_latent,
    cross_keep,
    latent_keep,
    residual_keep,
):
    seq_count = lax.axis_size("seq")
    seq_index = lax.axis_index("seq")
    head_index = lax.axis_index("head")
    model_width = context.shape[1]
    head_local = cross_keep.shape[0]
    latent_count = cross_keep.shape[1]
    head_dim = wq_cross.shape[1] // head_local
    columns = model_width // lax.axis_size("head")
    local_rows = latent_count // seq_count
    first_row = seq_index * local_rows

    def project(rows, weight):
        return jnp.dot(rows, weight, preferred_element_type=jnp.float32).astype(jnp.bfloat16)

    normed = rms_rows(context)
    own_queries = project(normed[context.shape[0] - latent_count :], wq_cross)
    own_columns = lax.dynamic_slice_in_dim(
        context[context.shape[0] - latent_count :], head_index * columns, columns, 1
    )
    own_columns = jnp.where(seq_index == seq_count - 1, own_columns, 0).astype(jnp.bfloat16)
    inputs = lax.psum_scatter(own_columns, "seq", scatter_dimension=0, tiled=True)
    key_rows = project(normed, wk_cross)
    value_rows = project(normed, wv_cross)
    queries = spread(own_queries, "seq", 1)
    partial, stats = cross_attention(
        queries, key_rows, value_rows, cross_keep, seq_count, head_dim
    )
    packed_stats = stats[:, :8].reshape(seq_count, local_rows, 8).transpose(0, 2, 1)
    partials, levels = exchange(
        [partial.reshape(seq_count, local_rows, head_local * head_dim), packed_stats],
        ["lead", "lead"],
        "seq",
        2,
    )
    levels = levels[:, :head_local, :]
    level_top = jnp.max(levels, axis=0, keepdims=True)
    share = jnp.exp(levels - level_top)
    share = share / jnp.sum(share, axis=0, keepdims=True)
    share = share.transpose(0, 2, 1)[..., None]
    spread_heads = partials.reshape(seq_count, local_rows, head_local, head_dim)
    attended = (
        jnp.sum(spread_heads.astype(jnp.float32) * share, axis=0)
        .reshape(local_rows, head_local * head_dim)
        .astype(jnp.bfloat16)
    )
    residual_rows = lax.dynamic_slice_in_dim(residual_keep, first_row, local_rows, 1)
    residual_mask = lax.dynamic_slice_in_dim(
        unpack_bits(residual_rows, 16), head_index * columns, columns, 2
    ).astype(jnp.float32)
    branches = exchange([project(attended, wo_cross)], ["cols"], "head", 3)[0]
    branch = jnp.sum(branches.astype(jnp.float32), axis=0)
    latents = (
        inputs.astype(jnp.float32) + residual_mask[0] * keep_scale * branch
    ).astype(jnp.bfloat16)
    gathered = exchange([latents], ["all"], "head", 4)[0]
    whole_latents = gathered.transpose(1, 0, 2).reshape(local_rows, model_width)
    normed_latents = rms_rows(whole_latents)
    latent_queries = project(normed_latents, wq_latent)
    latent_keys = project(normed_latents, wk_latent)
    latent_values = project(normed_latents, wv_latent)
    latent_words = lax.dynamic_slice_in_dim(latent_keep, first_row, local_rows, 1)
    all_keys, all_values = exchange([latent_keys, latent_values], ["all", "all"], "seq", 5)
    latent_attended = latent_attention(
        latent_queries, all_keys, all_values, latent_words, head_dim
    )
    latent_branches = exchange([project(latent_attended, wo_latent)], ["cols"], "head", 6)[0]
    latent_branch = jnp.sum(latent_branches.astype(jnp.float32), axis=0)
    return (latents.astype(jnp.float32) + residual_mask[1] * keep_scale * latent_branch).astype(
        jnp.bfloat16
    )


def solution(mesh):
    in_specs = (
        P("seq", None),
        P(None, "head"),
        P(None, "head"),
        P(None, "head"),
        P("head", None),
        P(None, "head"),
        P(None, "head"),
        P(None, "head"),
        P("head", None),
        P("head", None, "seq"),
        P("head", None, None),
        P(),
    )
    out_specs = P("seq", "head")
    return jax.shard_map(
        per_device, mesh=mesh, in_specs=in_specs, out_specs=out_specs, check_vma=False
    )
```

```python
import functools
import math

import jax
import jax.numpy as jnp
from jax import lax
from jax.experimental import pallas as pl
from jax.experimental.pallas import tpu as pltpu
from jax.sharding import PartitionSpec as P

keep_scale = 8.0 / 7.0
masked = -1e30
log2e = 1.4426950408889634
MESH = pl.DeviceIdType.MESH
ANY = pl.BlockSpec(memory_space=pl.ANY)


def rms_rows(matrix):
    wide_rows = matrix.astype(jnp.float32)
    mean_square = jnp.mean(wide_rows * wide_rows, axis=-1, keepdims=True)
    return (wide_rows * lax.rsqrt(mean_square + 1e-06)).astype(jnp.bfloat16)


def greet(axis, n, me):
    barrier = pltpu.get_barrier_semaphore()
    for d in range(1, n):
        pl.semaphore_signal(
            barrier, inc=1, device_id={axis: lax.rem(me + d, n)}, device_id_type=MESH
        )
    pl.semaphore_wait(barrier, n - 1)


def exchange_kernel(axis, n, modes, widths, *refs):
    count = len(modes)
    ins, outs = refs[:count], refs[count : 2 * count]
    send_sem, recv_sem, local_sem = refs[2 * count :]
    me = lax.axis_index(axis)

    def piece(a, j):
        if modes[a] == "lead":
            return ins[a].at[j]
        if modes[a] == "cols":
            start = pl.multiple_of(j * widths[a], 128)
            return ins[a].at[:, pl.ds(start, widths[a])]
        return ins[a]

    def place(a):
        if modes[a] == "beside":
            return outs[a].at[:, pl.ds(pl.multiple_of(me * widths[a], 128), widths[a])]
        return outs[a].at[me]

    local = []
    for a in range(count):
        copy = pltpu.make_async_copy(piece(a, me), place(a), local_sem.at[a])
        copy.start()
        local.append(copy)
    greet(axis, n, me)
    copies = []
    for d in range(1, n):
        to = lax.rem(me + d, n)
        for a in range(count):
            copy = pltpu.make_async_remote_copy(
                src_ref=piece(a, to),
                dst_ref=place(a),
                send_sem=send_sem.at[a, d],
                recv_sem=recv_sem.at[a, d],
                device_id={axis: to},
                device_id_type=MESH,
            )
            copy.start()
            copies.append(copy)
    for copy in copies:
        copy.wait()
    for copy in local:
        copy.wait()


def exchange(arrays, modes, axis, ident):
    n = lax.axis_size(axis)
    shapes, widths = [], []
    for x, mode in zip(arrays, modes):
        if mode == "lead":
            shape, width = x.shape, 0
        elif mode == "cols":
            width = x.shape[1] // n
            shape = (n, x.shape[0], width)
        else:
            shape, width = (x.shape[0], n * x.shape[1]), x.shape[1]
        shapes.append(jax.ShapeDtypeStruct(shape, x.dtype))
        widths.append(width)
    return pl.pallas_call(
        functools.partial(exchange_kernel, axis, n, tuple(modes), tuple(widths)),
        out_shape=tuple(shapes),
        in_specs=[ANY] * len(arrays),
        out_specs=tuple([ANY] * len(arrays)),
        scratch_shapes=[
            pltpu.SemaphoreType.DMA((len(arrays), n)),
            pltpu.SemaphoreType.DMA((len(arrays), n)),
            pltpu.SemaphoreType.DMA((len(arrays),)),
        ],
        compiler_params=pltpu.CompilerParams(collective_id=ident, has_side_effects=True),
    )(*arrays)


def spread_kernel(axis, n, across, chunks, x_ref, out_ref, send_sem, recv_sem, local_sem):
    me = lax.axis_index(axis)
    down = n // across
    z, x = me // across, lax.rem(me, across)
    root = me == n - 1
    greet(axis, n, me)
    first = x == across - 1
    top, below = z == down - 1, z == down - 2
    inner = jnp.logical_and
    children = (
        (
            (inner(first, z > 0), me - across),
            (inner(jnp.logical_not(top), x > 0), me - 1),
            (inner(below, jnp.logical_not(first)), me + across),
        ),
        (
            (inner(top, x > 0), me - 1),
            (inner(x == 0, z > 0), me - across),
            (inner(jnp.logical_not(top), jnp.logical_not(first)), me + 1),
        ),
    )

    def remote(ref, flow, c, child, to):
        at = flow * chunks + c
        return pltpu.make_async_remote_copy(
            src_ref=ref.at[at],
            dst_ref=out_ref.at[at],
            send_sem=send_sem.at[child, at],
            recv_sem=recv_sem.at[at],
            device_id={axis: to},
            device_id_type=MESH,
        )

    @pl.when(root)
    def _():
        own = pltpu.make_async_copy(x_ref, out_ref, local_sem)
        own.start()
        copies = []
        for c in range(chunks):
            copies.append(remote(x_ref, 0, c, 0, me - across))
            copies[-1].start()
            copies.append(remote(x_ref, 1, c, 0, me - 1))
            copies[-1].start()
        for copy in copies:
            copy.wait_send()
        own.wait()

    @pl.when(jnp.logical_not(root))
    def _():
        for c in range(chunks):
            for flow in range(2):
                remote(out_ref, flow, c, 0, n - 1).wait_recv()
                for child, (there, to) in enumerate(children[flow]):

                    @pl.when(there)
                    def _():
                        remote(out_ref, flow, c, child, to).start()

        for flow in range(2):
            for child, (there, to) in enumerate(children[flow]):

                @pl.when(there)
                def _():
                    for c in range(chunks):
                        remote(out_ref, flow, c, child, to).wait_send()


def spread(x, axis, ident):
    n = lax.axis_size(axis)
    rows, width = x.shape
    across = max(d for d in range(1, n) if n % d == 0 and d * d <= n)
    chunks = 8
    grains = x.reshape(2 * chunks, rows // (2 * chunks), width)
    out = pl.pallas_call(
        functools.partial(spread_kernel, axis, n, across, chunks),
        out_shape=jax.ShapeDtypeStruct(grains.shape, x.dtype),
        in_specs=[ANY],
        out_specs=ANY,
        scratch_shapes=[
            pltpu.SemaphoreType.DMA((3, 2 * chunks)),
            pltpu.SemaphoreType.DMA((2 * chunks,)),
            pltpu.SemaphoreType.DMA,
        ],
        compiler_params=pltpu.CompilerParams(collective_id=ident, has_side_effects=True),
    )(grains)
    return out.reshape(rows, width)


def piece_of(slot, sub, g):
    return slot * g + (sub if slot % 2 == 0 else g - 1 - sub)


def owner_of(me, g):
    slot, place = me // g, lax.rem(me, g)
    return slot, jnp.where(lax.rem(slot, 2) == 0, place, g - 1 - place)


def deal_kernel(axis, n, heads, hd, *refs):
    q_ref, k_ref, v_ref, qo, ko, vo, send, recv, qsend, qrecv, local = refs
    me = lax.axis_index(axis)
    g = n // heads

    def cut(ref, j):
        return ref.at[:, pl.ds(pl.multiple_of((j // g) * hd, 128), hd)]

    own = [
        pltpu.make_async_copy(cut(k_ref, me), ko.at[me], local.at[0]),
        pltpu.make_async_copy(cut(v_ref, me), vo.at[me], local.at[1]),
    ]
    for copy in own:
        copy.start()
    slot, sub = owner_of(me, g)

    def query(h):
        to = h * g + sub
        return to, pltpu.make_async_remote_copy(
            src_ref=q_ref.at[:, h * hd : (h + 1) * hd],
            dst_ref=qo.at[slot],
            send_sem=qsend.at[h],
            recv_sem=qrecv.at[slot],
            device_id={axis: to},
            device_id_type=MESH,
        )

    greet(axis, n, me)
    copies = []
    for d in range(1, n):
        to = lax.rem(me + d, n)
        for a, (ref, out) in enumerate(((k_ref, ko), (v_ref, vo))):
            copies.append(
                pltpu.make_async_remote_copy(
                    src_ref=cut(ref, to),
                    dst_ref=out.at[me],
                    send_sem=send.at[a, d],
                    recv_sem=recv.at[a, d],
                    device_id={axis: to},
                    device_id_type=MESH,
                )
            )
            copies[-1].start()
    for h in range(heads):
        to, copy = query(h)

        @pl.when(to != me)
        def _():
            copy.start()

        @pl.when(to == me)
        def _():
            mine = pltpu.make_async_copy(
                q_ref.at[:, h * hd : (h + 1) * hd], qo.at[slot], local.at[2]
            )
            mine.start()
            mine.wait()

    for copy in copies:
        copy.wait()
    for h in range(heads):
        to, copy = query(h)

        @pl.when(to != me)
        def _():
            copy.wait_send()

    for t in range(heads):
        source = piece_of(t, lax.rem(me, g), g)

        @pl.when(source != me)
        def _():
            pltpu.make_async_remote_copy(
                src_ref=qo.at[t],
                dst_ref=qo.at[t],
                send_sem=qsend.at[t],
                recv_sem=qrecv.at[t],
                device_id={axis: source},
                device_id_type=MESH,
            ).wait_recv()

    for copy in own:
        copy.wait()


def deal(queries, keys, values, axis, hd, ident):
    n = lax.axis_size(axis)
    rows, width = queries.shape
    heads = width // hd
    whole = jax.ShapeDtypeStruct((n, rows, hd), keys.dtype)
    return pl.pallas_call(
        functools.partial(deal_kernel, axis, n, heads, hd),
        out_shape=(jax.ShapeDtypeStruct((heads, rows, hd), queries.dtype), whole, whole),
        in_specs=[ANY] * 3,
        out_specs=(ANY,) * 3,
        scratch_shapes=[
            pltpu.SemaphoreType.DMA((2, n)),
            pltpu.SemaphoreType.DMA((2, n)),
            pltpu.SemaphoreType.DMA((heads,)),
            pltpu.SemaphoreType.DMA((heads,)),
            pltpu.SemaphoreType.DMA((3,)),
        ],
        compiler_params=pltpu.CompilerParams(collective_id=ident, has_side_effects=True),
    )(queries, keys, values)


def collect_kernel(axis, n, heads, hd, x_ref, out_ref, send, recv, local):
    me = lax.axis_index(axis)
    g = n // heads
    head = me // g
    cols = pl.ds(pl.multiple_of(head * hd, 128), hd)
    greet(axis, n, me)

    def outgoing(t):
        to = piece_of(t, lax.rem(me, g), g)
        return to, pltpu.make_async_remote_copy(
            src_ref=x_ref.at[t],
            dst_ref=out_ref.at[:, cols],
            send_sem=send.at[t],
            recv_sem=recv.at[head],
            device_id={axis: to},
            device_id_type=MESH,
        )

    for t in range(heads):
        to, copy = outgoing(t)

        @pl.when(to != me)
        def _():
            copy.start()

        @pl.when(to == me)
        def _():
            mine = pltpu.make_async_copy(x_ref.at[t], out_ref.at[:, cols], local)
            mine.start()
            mine.wait()

    for t in range(heads):
        to, copy = outgoing(t)

        @pl.when(to != me)
        def _():
            copy.wait_send()

    slot, sub = owner_of(me, g)
    for h in range(heads):
        source = h * g + sub

        @pl.when(source != me)
        def _():
            pltpu.make_async_remote_copy(
                src_ref=x_ref.at[0],
                dst_ref=out_ref.at[:, h * hd : (h + 1) * hd],
                send_sem=send.at[0],
                recv_sem=recv.at[h],
                device_id={axis: source},
                device_id_type=MESH,
            ).wait_recv()


def collect(x, axis, ident):
    n = lax.axis_size(axis)
    heads, rows, hd = x.shape
    return pl.pallas_call(
        functools.partial(collect_kernel, axis, n, heads, hd),
        out_shape=jax.ShapeDtypeStruct((rows, heads * hd), x.dtype),
        in_specs=[ANY],
        out_specs=ANY,
        scratch_shapes=[
            pltpu.SemaphoreType.DMA((heads,)),
            pltpu.SemaphoreType.DMA((heads,)),
            pltpu.SemaphoreType.DMA,
        ],
        compiler_params=pltpu.CompilerParams(collective_id=ident, has_side_effects=True),
    )(x)


def dot_t(a, b):
    return lax.dot_general(a, b, (((1,), (1,)), ((), ())), preferred_element_type=jnp.float32)


def fold_lanes(x, op):
    parts = [x[:, j : j + 128] for j in range(0, x.shape[1], 128)]
    return functools.reduce(op, parts)


def cross_kernel(n, hd, scale, q_ref, k_ref, v_ref, w_ref, o_ref, st_ref, s_ref):
    block, head = pl.program_id(0), pl.program_id(1)
    bq = q_ref.shape[0]
    keys = k_ref.shape[0]
    chunk = w_ref.shape[2]
    chunks = keys // chunk
    root = lax.axis_index("seq") == n - 1
    cols = pl.ds(pl.multiple_of(head * hd, 128), hd)
    factor = scale * log2e

    def finish(acc, top, total):
        o_ref[...] = (acc * (keep_scale / total)).astype(o_ref.dtype)
        stat = top * scale + jnp.log(total)
        lane = lax.broadcasted_iota(jnp.int32, st_ref.shape, 1)
        st_ref[...] = jnp.where(lane == head, stat, st_ref[...])

    @pl.when(head == 0)
    def _():
        st_ref[...] = jnp.zeros_like(st_ref)

    @pl.when(jnp.logical_not(root))
    def _():
        q = q_ref[...]
        tops = None
        for c in range(chunks):
            s = dot_t(q, k_ref[c * chunk : (c + 1) * chunk, cols])
            s_ref[c] = s
            t = fold_lanes(s, jnp.maximum)
            tops = t if tops is None else jnp.maximum(tops, t)
        top = jnp.max(tops, axis=1, keepdims=True)
        words = w_ref[0]
        acc = jnp.zeros((bq, hd), jnp.float32)
        sums = jnp.zeros((bq, 128), jnp.float32)
        for c in range(chunks):
            e = jnp.exp2((s_ref[c] - top) * factor)
            sums = sums + fold_lanes(e, jnp.add)
            weights = jnp.where((words & (1 << c)) != 0, e, 0.0).astype(jnp.bfloat16)
            acc = acc + jnp.dot(
                weights,
                v_ref[c * chunk : (c + 1) * chunk, cols],
                preferred_element_type=jnp.float32,
            )
        finish(acc, top, jnp.sum(sums, axis=1, keepdims=True))

    @pl.when(root)
    def _():
        q = q_ref[...]
        used = jnp.minimum(((block + 1) * bq + chunk - 1) // chunk, chunks)
        row = block * bq + lax.broadcasted_iota(jnp.int32, (bq, chunk), 0)
        lane = lax.broadcasted_iota(jnp.int32, (bq, chunk), 1)

        def first(c, tops):
            at = pl.ds(pl.multiple_of(c * chunk, chunk), chunk)
            s = dot_t(q, k_ref[at, cols])
            s = jnp.where(lane + c * chunk <= row, s, masked)
            s_ref[c] = s
            return jnp.maximum(tops, fold_lanes(s, jnp.maximum))

        tops = lax.fori_loop(0, used, first, jnp.full((bq, 128), masked, jnp.float32))
        top = jnp.max(tops, axis=1, keepdims=True)
        words = w_ref[0]

        def second(c, carry):
            acc, sums = carry
            at = pl.ds(pl.multiple_of(c * chunk, chunk), chunk)
            e = jnp.exp2((s_ref[c] - top) * factor)
            e = jnp.where(lane + c * chunk <= row, e, 0.0)
            sums = sums + fold_lanes(e, jnp.add)
            weights = jnp.where((words & (1 << c)) != 0, e, 0.0).astype(jnp.bfloat16)
            acc = acc + jnp.dot(weights, v_ref[at, cols], preferred_element_type=jnp.float32)
            return acc, sums

        acc, sums = lax.fori_loop(
            0,
            used,
            second,
            (jnp.zeros((bq, hd), jnp.float32), jnp.zeros((bq, 128), jnp.float32)),
        )
        finish(acc, top, jnp.sum(sums, axis=1, keepdims=True))


def cross_attention(queries, keys, values, words, n, hd):
    rows, width = queries.shape
    toks = keys.shape[0]
    heads = width // hd
    bq = min(256, rows)
    chunk = words.shape[2]
    return pl.pallas_call(
        functools.partial(cross_kernel, n, hd, 1.0 / math.sqrt(hd)),
        grid=(rows // bq, heads),
        in_specs=[
            pl.BlockSpec((bq, hd), lambda i, h: (i, h)),
            pl.BlockSpec((toks, width), lambda i, h: (0, 0)),
            pl.BlockSpec((toks, width), lambda i, h: (0, 0)),
            pl.BlockSpec((1, bq, chunk), lambda i, h: (h, i, 0)),
        ],
        out_specs=(
            pl.BlockSpec((bq, hd), lambda i, h: (i, h)),
            pl.BlockSpec((bq, 128), lambda i, h: (i, 0)),
        ),
        out_shape=(
            jax.ShapeDtypeStruct((rows, width), jnp.bfloat16),
            jax.ShapeDtypeStruct((rows, 128), jnp.float32),
        ),
        scratch_shapes=[pltpu.VMEM((toks // chunk, bq, chunk), jnp.float32)],
        cost_estimate=pl.CostEstimate(
            flops=4 * rows * toks * width * 4,
            transcendentals=heads * rows * toks,
            bytes_accessed=4 * heads * rows * chunk,
        ),
    )(queries, keys, values, words)


def latent_kernel(hd, scale, at_ref, q_ref, k_ref, v_ref, w_ref, o_ref, s_ref):
    rows = q_ref.shape[1]
    pieces, piece_rows = k_ref.shape[0], k_ref.shape[1]
    chunk = w_ref.shape[2]
    factor = scale * log2e
    row = at_ref[1 + pl.program_id(0)] * rows + lax.broadcasted_iota(jnp.int32, (rows, chunk), 0)
    lane = lax.broadcasted_iota(jnp.int32, (rows, chunk), 1)
    per = piece_rows // chunk
    q = q_ref[0]
    words = w_ref[0]
    tops = jnp.full((rows, 128), masked, jnp.float32)
    for p in range(pieces):
        s = dot_t(q, k_ref[p])
        for j in range(per):
            c = p * per + j
            part = jnp.where(lane + c * chunk <= row, s[:, j * chunk : (j + 1) * chunk], masked)
            s_ref[c] = part
            tops = jnp.maximum(tops, part)
    top = jnp.max(tops, axis=1, keepdims=True)
    acc = jnp.zeros((rows, hd), jnp.float32)
    sums = jnp.zeros((rows, 128), jnp.float32)
    for p in range(pieces):
        kept = []
        for j in range(per):
            c = p * per + j
            e = jnp.exp2((s_ref[c] - top) * factor)
            e = jnp.where(lane + c * chunk <= row, e, 0.0)
            sums = sums + e
            kept.append(jnp.where((words & (1 << c)) != 0, e, 0.0).astype(jnp.bfloat16))
        weights = jnp.concatenate(kept, axis=1) if per > 1 else kept[0]
        acc = acc + jnp.dot(weights, v_ref[p], preferred_element_type=jnp.float32)
    total = jnp.sum(sums, axis=1, keepdims=True)
    o_ref[0] = (acc * (keep_scale / total)).astype(o_ref.dtype)


def latent_attention(places, queries, keys, values, words):
    slots, rows, hd = queries.shape
    pieces, piece_rows, _ = keys.shape
    chunk = words.shape[2]
    return pl.pallas_call(
        functools.partial(latent_kernel, hd, 1.0 / math.sqrt(hd)),
        grid_spec=pltpu.PrefetchScalarGridSpec(
            num_scalar_prefetch=1,
            grid=(slots,),
            in_specs=[
                pl.BlockSpec((1, rows, hd), lambda t, at: (t, 0, 0)),
                pl.BlockSpec((pieces, piece_rows, hd), lambda t, at: (0, 0, 0)),
                pl.BlockSpec((pieces, piece_rows, hd), lambda t, at: (0, 0, 0)),
                pl.BlockSpec((1, rows, chunk), lambda t, at: (at[0], at[1 + t], 0)),
            ],
            out_specs=pl.BlockSpec((1, rows, hd), lambda t, at: (t, 0, 0)),
            scratch_shapes=[
                pltpu.VMEM((pieces * piece_rows // chunk, rows, chunk), jnp.float32)
            ],
        ),
        out_shape=jax.ShapeDtypeStruct(queries.shape, jnp.bfloat16),
    )(places, queries, keys, values, words)


def combine_kernel(n, heads, hd, stride, p_ref, level_ref, w_ref, o_ref):
    levels = level_ref[...]
    parts = []
    for h in range(heads):
        mine = [levels[:, s * stride + h : s * stride + h + 1] for s in range(n)]
        top = functools.reduce(jnp.maximum, mine)
        shares = [jnp.exp(level - top) for level in mine]
        total = functools.reduce(jnp.add, shares)
        acc = None
        for s in range(n):
            term = p_ref[s, :, h * hd : (h + 1) * hd].astype(jnp.float32) * shares[s]
            acc = term if acc is None else acc + term
        parts.append((acc / total).astype(jnp.bfloat16))
    attended = jnp.concatenate(parts, axis=1)
    o_ref[...] = jnp.dot(attended, w_ref[...], preferred_element_type=jnp.float32).astype(
        jnp.bfloat16
    )


def combine(partials, levels, weight, heads, hd):
    n, rows, _ = partials.shape
    stride = levels.shape[1] // n
    return pl.pallas_call(
        functools.partial(combine_kernel, n, heads, hd, stride),
        out_shape=jax.ShapeDtypeStruct((rows, weight.shape[1]), jnp.bfloat16),
    )(partials, levels, weight)


def per_device(
    context,
    wq_cross,
    wk_cross,
    wv_cross,
    wo_cross,
    wq_latent,
    wk_latent,
    wv_latent,
    wo_latent,
    cross_keep,
    latent_keep,
    residual_keep,
):
    seq_count = lax.axis_size("seq")
    seq_index = lax.axis_index("seq")
    head_index = lax.axis_index("head")
    model_width = context.shape[1]
    head_local = cross_keep.shape[0]
    latent_count = cross_keep.shape[1]
    head_dim = wq_cross.shape[1] // head_local
    columns = model_width // lax.axis_size("head")
    local_rows = latent_count // seq_count
    first_row = seq_index * local_rows

    def project(rows, weight):
        return jnp.dot(rows, weight, preferred_element_type=jnp.float32).astype(jnp.bfloat16)

    normed = rms_rows(context)
    own_queries = project(normed[context.shape[0] - latent_count :], wq_cross)
    queries = spread(own_queries, "seq", 1)
    own_columns = lax.dynamic_slice_in_dim(
        context[context.shape[0] - latent_count :], head_index * columns, columns, 1
    )
    own_columns = jnp.where(seq_index == seq_count - 1, own_columns, 0).astype(jnp.bfloat16)
    own_columns, queries = lax.optimization_barrier((own_columns, queries))
    inputs = lax.psum_scatter(own_columns, "seq", scatter_dimension=0, tiled=True)
    key_rows = project(normed, wk_cross)
    value_rows = project(normed, wv_cross)
    partial, stats = cross_attention(
        queries, key_rows, value_rows, cross_keep, seq_count, head_dim
    )
    packed_stats = stats[:, :8].reshape(seq_count, local_rows, 8).transpose(0, 2, 1)
    partials, levels = exchange(
        [partial.reshape(seq_count, local_rows, head_local * head_dim), packed_stats],
        ["lead", "lead"],
        "seq",
        2,
    )
    levels = levels.reshape(seq_count * 8, local_rows).T
    own_branch = combine(partials, levels, wo_cross, head_local, head_dim)
    branches = exchange([own_branch], ["cols"], "head", 3)[0]
    words = lax.dynamic_slice_in_dim(residual_keep, first_row, local_rows, 1)
    blocks = columns // words.shape[2]
    flags = jnp.concatenate(
        [jnp.right_shift(words, head_index * blocks + b) & 1 for b in range(blocks)], axis=2
    ).astype(jnp.float32)
    branch = jnp.sum(branches.astype(jnp.float32), axis=0)
    latents = (inputs.astype(jnp.float32) + flags[0] * keep_scale * branch).astype(jnp.bfloat16)
    normed_latents = rms_rows(exchange([latents], ["beside"], "head", 4)[0])
    latent_queries = project(normed_latents, wq_latent)
    latent_keys = project(normed_latents, wk_latent)
    latent_values = project(normed_latents, wv_latent)
    dealt_queries, dealt_keys, dealt_values = deal(
        latent_queries, latent_keys, latent_values, "seq", head_dim, 5
    )
    group = seq_count // head_local
    places = jnp.stack(
        [seq_index // group]
        + [piece_of(t, lax.rem(seq_index, group), group) for t in range(head_local)]
    ).astype(jnp.int32)
    dealt_out = latent_attention(places, dealt_queries, dealt_keys, dealt_values, latent_keep)
    latent_attended = collect(dealt_out, "seq", 7)
    latent_branches = exchange([project(latent_attended, wo_latent)], ["cols"], "head", 6)[0]
    latent_branch = jnp.sum(latent_branches.astype(jnp.float32), axis=0)
    return (latents.astype(jnp.float32) + flags[1] * keep_scale * latent_branch).astype(
        jnp.bfloat16
    )


def solution(mesh):
    in_specs = (
        P("seq", None),
        P(None, "head"),
        P(None, "head"),
        P(None, "head"),
        P("head", None),
        P(None, "head"),
        P(None, "head"),
        P(None, "head"),
        P("head", None),
        P("head", None, "seq"),
        P("head", None, None),
        P(),
    )
    out_specs = P("seq", "head")
    return jax.shard_map(
        per_device, mesh=mesh, in_specs=in_specs, out_specs=out_specs, check_vma=False
    )
```

```python
import functools
import math

import jax
import jax.numpy as jnp
from jax import lax
from jax.experimental import pallas as pl
from jax.experimental.pallas import tpu as pltpu
from jax.sharding import PartitionSpec as P

keep_scale = 8.0 / 7.0
masked = -1e30
log2e = 1.4426950408889634
MESH = pl.DeviceIdType.MESH
ANY = pl.BlockSpec(memory_space=pl.ANY)


def rms_rows(matrix):
    wide_rows = matrix.astype(jnp.float32)
    mean_square = jnp.mean(wide_rows * wide_rows, axis=-1, keepdims=True)
    return (wide_rows * lax.rsqrt(mean_square + 1e-06)).astype(jnp.bfloat16)


def greet(axis, n, me):
    barrier = pltpu.get_barrier_semaphore()
    for d in range(1, n):
        pl.semaphore_signal(
            barrier, inc=1, device_id={axis: lax.rem(me + d, n)}, device_id_type=MESH
        )
    pl.semaphore_wait(barrier, n - 1)


def relay(src, buffer, dst, sem):
    inward = pltpu.make_async_copy(src, buffer, sem)
    inward.start()
    inward.wait()
    outward = pltpu.make_async_copy(buffer, dst, sem)
    outward.start()
    return outward


def exchange_kernel(axis, n, modes, widths, *refs):
    count = len(modes)
    ins, outs = refs[:count], refs[count : 2 * count]
    send_sem, recv_sem, local_sem = refs[2 * count : 2 * count + 3]
    buffers = refs[2 * count + 3 :]
    me = lax.axis_index(axis)

    def piece(a, j):
        if modes[a] == "lead":
            return ins[a].at[j]
        if modes[a] == "cols":
            start = pl.multiple_of(j * widths[a], 128)
            return ins[a].at[:, pl.ds(start, widths[a])]
        return ins[a]

    def place(a):
        if modes[a] == "beside":
            return outs[a].at[:, pl.ds(pl.multiple_of(me * widths[a], 128), widths[a])]
        return outs[a].at[me]

    greet(axis, n, me)
    copies = []
    for d in range(1, n):
        to = lax.rem(me + d, n)
        for a in range(count):
            copy = pltpu.make_async_remote_copy(
                src_ref=piece(a, to),
                dst_ref=place(a),
                send_sem=send_sem.at[a, d],
                recv_sem=recv_sem.at[a, d],
                device_id={axis: to},
                device_id_type=MESH,
            )
            copy.start()
            copies.append(copy)
    for a in range(count):
        copies.append(relay(piece(a, me), buffers[a], place(a), local_sem.at[a]))
    for copy in copies:
        copy.wait()


def exchange(arrays, modes, axis, ident):
    n = lax.axis_size(axis)
    shapes, widths, buffers = [], [], []
    for x, mode in zip(arrays, modes):
        if mode == "lead":
            shape, width = x.shape, 0
            own = x.shape[1:]
        elif mode == "cols":
            width = x.shape[1] // n
            shape = (n, x.shape[0], width)
            own = shape[1:]
        else:
            shape, width = (x.shape[0], n * x.shape[1]), x.shape[1]
            own = x.shape
        shapes.append(jax.ShapeDtypeStruct(shape, x.dtype))
        widths.append(width)
        buffers.append(pltpu.VMEM(own, x.dtype))
    return pl.pallas_call(
        functools.partial(exchange_kernel, axis, n, tuple(modes), tuple(widths)),
        out_shape=tuple(shapes),
        in_specs=[ANY] * len(arrays),
        out_specs=tuple([ANY] * len(arrays)),
        scratch_shapes=[
            pltpu.SemaphoreType.DMA((len(arrays), n)),
            pltpu.SemaphoreType.DMA((len(arrays), n)),
            pltpu.SemaphoreType.DMA((len(arrays),)),
        ]
        + buffers,
        compiler_params=pltpu.CompilerParams(collective_id=ident, has_side_effects=True),
    )(*arrays)


def spread_kernel(axis, n, across, chunks, x_ref, out_ref, send_sem, recv_sem):
    me = lax.axis_index(axis)
    down = n // across
    z, x = me // across, lax.rem(me, across)
    root = me == n - 1
    greet(axis, n, me)
    first = x == across - 1
    top, below = z == down - 1, z == down - 2
    inner = jnp.logical_and
    children = (
        (
            (inner(first, z > 0), me - across),
            (inner(jnp.logical_not(top), x > 0), me - 1),
            (inner(below, jnp.logical_not(first)), me + across),
        ),
        (
            (inner(top, x > 0), me - 1),
            (inner(x == 0, z > 0), me - across),
            (inner(jnp.logical_not(top), jnp.logical_not(first)), me + 1),
        ),
    )

    def remote(ref, flow, c, child, to):
        at = flow * chunks + c
        return pltpu.make_async_remote_copy(
            src_ref=ref.at[at],
            dst_ref=out_ref.at[at],
            send_sem=send_sem.at[child, at],
            recv_sem=recv_sem.at[at],
            device_id={axis: to},
            device_id_type=MESH,
        )

    @pl.when(root)
    def _():
        copies = []
        for c in range(chunks):
            copies.append(remote(out_ref, 0, c, 0, me - across))
            copies[-1].start()
            copies.append(remote(out_ref, 1, c, 0, me - 1))
            copies[-1].start()
        for copy in copies:
            copy.wait_send()

    @pl.when(jnp.logical_not(root))
    def _():
        for c in range(chunks):
            for flow in range(2):
                remote(out_ref, flow, c, 0, n - 1).wait_recv()
                for child, (there, to) in enumerate(children[flow]):

                    @pl.when(there)
                    def _():
                        remote(out_ref, flow, c, child, to).start()

        for flow in range(2):
            for child, (there, to) in enumerate(children[flow]):

                @pl.when(there)
                def _():
                    for c in range(chunks):
                        remote(out_ref, flow, c, child, to).wait_send()


def spread(x, axis, ident):
    n = lax.axis_size(axis)
    rows, width = x.shape
    across = max(d for d in range(1, n) if n % d == 0 and d * d <= n)
    chunks = 16
    grains = x.reshape(2 * chunks, rows // (2 * chunks), width)
    out = pl.pallas_call(
        functools.partial(spread_kernel, axis, n, across, chunks),
        out_shape=jax.ShapeDtypeStruct(grains.shape, x.dtype),
        in_specs=[ANY],
        out_specs=ANY,
        input_output_aliases={0: 0},
        scratch_shapes=[
            pltpu.SemaphoreType.DMA((3, 2 * chunks)),
            pltpu.SemaphoreType.DMA((2 * chunks,)),
        ],
        compiler_params=pltpu.CompilerParams(collective_id=ident, has_side_effects=True),
    )(grains)
    return out.reshape(rows, width)


def piece_of(slot, sub, g):
    return slot * g + (sub if slot % 2 == 0 else g - 1 - sub)


def owner_of(me, g):
    slot, place = me // g, lax.rem(me, g)
    return slot, jnp.where(lax.rem(slot, 2) == 0, place, g - 1 - place)


def deal_kernel(axis, n, heads, hd, *refs):
    q_ref, k_ref, v_ref, qo, ko, vo, send, recv, qsend, qrecv, local, buffer = refs
    me = lax.axis_index(axis)
    g = n // heads

    def cut(ref, j):
        return ref.at[:, pl.ds(pl.multiple_of((j // g) * hd, 128), hd)]

    slot, sub = owner_of(me, g)

    def query(h):
        to = h * g + sub
        return to, pltpu.make_async_remote_copy(
            src_ref=q_ref.at[:, h * hd : (h + 1) * hd],
            dst_ref=qo.at[slot],
            send_sem=qsend.at[h],
            recv_sem=qrecv.at[slot],
            device_id={axis: to},
            device_id_type=MESH,
        )

    greet(axis, n, me)
    copies = []
    for d in range(1, n):
        to = lax.rem(me + d, n)
        for a, (ref, out) in enumerate(((k_ref, ko), (v_ref, vo))):
            copies.append(
                pltpu.make_async_remote_copy(
                    src_ref=cut(ref, to),
                    dst_ref=out.at[me],
                    send_sem=send.at[a, d],
                    recv_sem=recv.at[a, d],
                    device_id={axis: to},
                    device_id_type=MESH,
                )
            )
            copies[-1].start()
    for h in range(heads):
        to, copy = query(h)

        @pl.when(to != me)
        def _():
            copy.start()

        @pl.when(to == me)
        def _():
            relay(
                q_ref.at[:, h * hd : (h + 1) * hd], buffer.at[2], qo.at[slot], local.at[2]
            ).wait()

    copies.append(relay(cut(k_ref, me), buffer.at[0], ko.at[me], local.at[0]))
    copies.append(relay(cut(v_ref, me), buffer.at[1], vo.at[me], local.at[1]))
    for copy in copies:
        copy.wait()
    for h in range(heads):
        to, copy = query(h)

        @pl.when(to != me)
        def _():
            copy.wait_send()

    for t in range(heads):
        source = piece_of(t, lax.rem(me, g), g)

        @pl.when(source != me)
        def _():
            pltpu.make_async_remote_copy(
                src_ref=qo.at[t],
                dst_ref=qo.at[t],
                send_sem=qsend.at[t],
                recv_sem=qrecv.at[t],
                device_id={axis: source},
                device_id_type=MESH,
            ).wait_recv()


def deal(queries, keys, values, axis, hd, ident):
    n = lax.axis_size(axis)
    rows, width = queries.shape
    heads = width // hd
    whole = jax.ShapeDtypeStruct((n, rows, hd), keys.dtype)
    return pl.pallas_call(
        functools.partial(deal_kernel, axis, n, heads, hd),
        out_shape=(jax.ShapeDtypeStruct((heads, rows, hd), queries.dtype), whole, whole),
        in_specs=[ANY] * 3,
        out_specs=(ANY,) * 3,
        scratch_shapes=[
            pltpu.SemaphoreType.DMA((2, n)),
            pltpu.SemaphoreType.DMA((2, n)),
            pltpu.SemaphoreType.DMA((heads,)),
            pltpu.SemaphoreType.DMA((heads,)),
            pltpu.SemaphoreType.DMA((3,)),
            pltpu.VMEM((3, rows, hd), keys.dtype),
        ],
        compiler_params=pltpu.CompilerParams(collective_id=ident, has_side_effects=True),
    )(queries, keys, values)


def collect_kernel(axis, n, heads, hd, x_ref, out_ref, send, recv, local, buffer):
    me = lax.axis_index(axis)
    g = n // heads
    head = me // g
    cols = pl.ds(pl.multiple_of(head * hd, 128), hd)
    greet(axis, n, me)

    def outgoing(t):
        to = piece_of(t, lax.rem(me, g), g)
        return to, pltpu.make_async_remote_copy(
            src_ref=x_ref.at[t],
            dst_ref=out_ref.at[:, cols],
            send_sem=send.at[t],
            recv_sem=recv.at[head],
            device_id={axis: to},
            device_id_type=MESH,
        )

    for t in range(heads):
        to, copy = outgoing(t)

        @pl.when(to != me)
        def _():
            copy.start()

        @pl.when(to == me)
        def _():
            relay(x_ref.at[t], buffer, out_ref.at[:, cols], local).wait()

    for t in range(heads):
        to, copy = outgoing(t)

        @pl.when(to != me)
        def _():
            copy.wait_send()

    slot, sub = owner_of(me, g)
    for h in range(heads):
        source = h * g + sub

        @pl.when(source != me)
        def _():
            pltpu.make_async_remote_copy(
                src_ref=x_ref.at[0],
                dst_ref=out_ref.at[:, h * hd : (h + 1) * hd],
                send_sem=send.at[0],
                recv_sem=recv.at[h],
                device_id={axis: source},
                device_id_type=MESH,
            ).wait_recv()


def collect(x, axis, ident):
    n = lax.axis_size(axis)
    heads, rows, hd = x.shape
    return pl.pallas_call(
        functools.partial(collect_kernel, axis, n, heads, hd),
        out_shape=jax.ShapeDtypeStruct((rows, heads * hd), x.dtype),
        in_specs=[ANY],
        out_specs=ANY,
        scratch_shapes=[
            pltpu.SemaphoreType.DMA((heads,)),
            pltpu.SemaphoreType.DMA((heads,)),
            pltpu.SemaphoreType.DMA,
            pltpu.VMEM((rows, hd), x.dtype),
        ],
        compiler_params=pltpu.CompilerParams(collective_id=ident, has_side_effects=True),
    )(x)


def dot_t(a, b):
    return lax.dot_general(a, b, (((1,), (1,)), ((), ())), preferred_element_type=jnp.float32)


def fold_lanes(x, op):
    parts = [x[:, j : j + 128] for j in range(0, x.shape[1], 128)]
    return functools.reduce(op, parts)


def cross_kernel(n, hd, scale, q_ref, k_ref, v_ref, w_ref, o_ref, st_ref, s_ref):
    block, head = pl.program_id(0), pl.program_id(1)
    bq = q_ref.shape[0]
    keys = k_ref.shape[0]
    chunk = w_ref.shape[2]
    chunks = keys // chunk
    root = lax.axis_index("seq") == n - 1
    cols = pl.ds(pl.multiple_of(head * hd, 128), hd)
    factor = scale * log2e

    def finish(acc, top, total):
        o_ref[...] = (acc * (keep_scale / total)).astype(o_ref.dtype)
        stat = top * scale + jnp.log(total)
        lane = lax.broadcasted_iota(jnp.int32, st_ref.shape, 1)
        st_ref[...] = jnp.where(lane == head, stat, st_ref[...])

    @pl.when(head == 0)
    def _():
        st_ref[...] = jnp.zeros_like(st_ref)

    @pl.when(jnp.logical_not(root))
    def _():
        q = q_ref[...]
        tops = None
        for c in range(chunks):
            s = dot_t(q, k_ref[c * chunk : (c + 1) * chunk, cols])
            s_ref[c] = s
            t = fold_lanes(s, jnp.maximum)
            tops = t if tops is None else jnp.maximum(tops, t)
        top = jnp.max(tops, axis=1, keepdims=True)
        words = w_ref[0]
        acc = jnp.zeros((bq, hd), jnp.float32)
        sums = jnp.zeros((bq, 128), jnp.float32)
        for c in range(chunks):
            e = jnp.exp2((s_ref[c] - top) * factor)
            sums = sums + fold_lanes(e, jnp.add)
            weights = jnp.where((words & (1 << c)) != 0, e, 0.0).astype(jnp.bfloat16)
            acc = acc + jnp.dot(
                weights,
                v_ref[c * chunk : (c + 1) * chunk, cols],
                preferred_element_type=jnp.float32,
            )
        finish(acc, top, jnp.sum(sums, axis=1, keepdims=True))

    @pl.when(root)
    def _():
        q = q_ref[...]
        used = jnp.minimum(((block + 1) * bq + chunk - 1) // chunk, chunks)
        row = block * bq + lax.broadcasted_iota(jnp.int32, (bq, chunk), 0)
        lane = lax.broadcasted_iota(jnp.int32, (bq, chunk), 1)

        def first(c, tops):
            at = pl.ds(pl.multiple_of(c * chunk, chunk), chunk)
            s = dot_t(q, k_ref[at, cols])
            s = jnp.where(lane + c * chunk <= row, s, masked)
            s_ref[c] = s
            return jnp.maximum(tops, fold_lanes(s, jnp.maximum))

        tops = lax.fori_loop(0, used, first, jnp.full((bq, 128), masked, jnp.float32))
        top = jnp.max(tops, axis=1, keepdims=True)
        words = w_ref[0]

        def second(c, carry):
            acc, sums = carry
            at = pl.ds(pl.multiple_of(c * chunk, chunk), chunk)
            e = jnp.exp2((s_ref[c] - top) * factor)
            e = jnp.where(lane + c * chunk <= row, e, 0.0)
            sums = sums + fold_lanes(e, jnp.add)
            weights = jnp.where((words & (1 << c)) != 0, e, 0.0).astype(jnp.bfloat16)
            acc = acc + jnp.dot(weights, v_ref[at, cols], preferred_element_type=jnp.float32)
            return acc, sums

        acc, sums = lax.fori_loop(
            0,
            used,
            second,
            (jnp.zeros((bq, hd), jnp.float32), jnp.zeros((bq, 128), jnp.float32)),
        )
        finish(acc, top, jnp.sum(sums, axis=1, keepdims=True))


def cross_attention(queries, keys, values, words, n, hd):
    rows, width = queries.shape
    toks = keys.shape[0]
    heads = width // hd
    bq = min(256, rows)
    chunk = words.shape[2]
    return pl.pallas_call(
        functools.partial(cross_kernel, n, hd, 1.0 / math.sqrt(hd)),
        grid=(rows // bq, heads),
        in_specs=[
            pl.BlockSpec((bq, hd), lambda i, h: (i, h)),
            pl.BlockSpec((toks, width), lambda i, h: (0, 0)),
            pl.BlockSpec((toks, width), lambda i, h: (0, 0)),
            pl.BlockSpec((1, bq, chunk), lambda i, h: (h, i, 0)),
        ],
        out_specs=(
            pl.BlockSpec((bq, hd), lambda i, h: (i, h)),
            pl.BlockSpec((bq, 128), lambda i, h: (i, 0)),
        ),
        out_shape=(
            jax.ShapeDtypeStruct((rows, width), jnp.bfloat16),
            jax.ShapeDtypeStruct((rows, 128), jnp.float32),
        ),
        scratch_shapes=[pltpu.VMEM((toks // chunk, bq, chunk), jnp.float32)],
        cost_estimate=pl.CostEstimate(
            flops=4 * rows * toks * width * 4,
            transcendentals=heads * rows * toks,
            bytes_accessed=4 * heads * rows * chunk,
        ),
    )(queries, keys, values, words)


def latent_kernel(hd, scale, at_ref, q_ref, k_ref, v_ref, w_ref, o_ref, s_ref):
    rows = q_ref.shape[1]
    pieces, piece_rows = k_ref.shape[0], k_ref.shape[1]
    chunk = w_ref.shape[2]
    factor = scale * log2e
    row = at_ref[1 + pl.program_id(0)] * rows + lax.broadcasted_iota(jnp.int32, (rows, chunk), 0)
    lane = lax.broadcasted_iota(jnp.int32, (rows, chunk), 1)
    per = piece_rows // chunk
    q = q_ref[0]
    words = w_ref[0]
    tops = jnp.full((rows, 128), masked, jnp.float32)
    for p in range(pieces):
        s = dot_t(q, k_ref[p])
        for j in range(per):
            c = p * per + j
            part = jnp.where(lane + c * chunk <= row, s[:, j * chunk : (j + 1) * chunk], masked)
            s_ref[c] = part
            tops = jnp.maximum(tops, part)
    top = jnp.max(tops, axis=1, keepdims=True)
    acc = jnp.zeros((rows, hd), jnp.float32)
    sums = jnp.zeros((rows, 128), jnp.float32)
    for p in range(pieces):
        kept = []
        for j in range(per):
            c = p * per + j
            e = jnp.exp2((s_ref[c] - top) * factor)
            e = jnp.where(lane + c * chunk <= row, e, 0.0)
            sums = sums + e
            kept.append(jnp.where((words & (1 << c)) != 0, e, 0.0).astype(jnp.bfloat16))
        weights = jnp.concatenate(kept, axis=1) if per > 1 else kept[0]
        acc = acc + jnp.dot(weights, v_ref[p], preferred_element_type=jnp.float32)
    total = jnp.sum(sums, axis=1, keepdims=True)
    o_ref[0] = (acc * (keep_scale / total)).astype(o_ref.dtype)


def latent_attention(places, queries, keys, values, words):
    slots, rows, hd = queries.shape
    pieces, piece_rows, _ = keys.shape
    chunk = words.shape[2]
    return pl.pallas_call(
        functools.partial(latent_kernel, hd, 1.0 / math.sqrt(hd)),
        grid_spec=pltpu.PrefetchScalarGridSpec(
            num_scalar_prefetch=1,
            grid=(slots,),
            in_specs=[
                pl.BlockSpec((1, rows, hd), lambda t, at: (t, 0, 0)),
                pl.BlockSpec((pieces, piece_rows, hd), lambda t, at: (0, 0, 0)),
                pl.BlockSpec((pieces, piece_rows, hd), lambda t, at: (0, 0, 0)),
                pl.BlockSpec((1, rows, chunk), lambda t, at: (at[0], at[1 + t], 0)),
            ],
            out_specs=pl.BlockSpec((1, rows, hd), lambda t, at: (t, 0, 0)),
            scratch_shapes=[
                pltpu.VMEM((pieces * piece_rows // chunk, rows, chunk), jnp.float32)
            ],
        ),
        out_shape=jax.ShapeDtypeStruct(queries.shape, jnp.bfloat16),
    )(places, queries, keys, values, words)


def combine_kernel(n, heads, hd, stride, p_ref, level_ref, w_ref, o_ref):
    levels = level_ref[...]
    parts = []
    for h in range(heads):
        mine = [levels[:, s * stride + h : s * stride + h + 1] for s in range(n)]
        top = functools.reduce(jnp.maximum, mine)
        shares = [jnp.exp(level - top) for level in mine]
        total = functools.reduce(jnp.add, shares)
        acc = None
        for s in range(n):
            term = p_ref[s, :, h * hd : (h + 1) * hd].astype(jnp.float32) * shares[s]
            acc = term if acc is None else acc + term
        parts.append((acc / total).astype(jnp.bfloat16))
    attended = jnp.concatenate(parts, axis=1)
    o_ref[...] = jnp.dot(attended, w_ref[...], preferred_element_type=jnp.float32).astype(
        jnp.bfloat16
    )


def combine(partials, levels, weight, heads, hd):
    n, rows, _ = partials.shape
    stride = levels.shape[1] // n
    return pl.pallas_call(
        functools.partial(combine_kernel, n, heads, hd, stride),
        out_shape=jax.ShapeDtypeStruct((rows, weight.shape[1]), jnp.bfloat16),
    )(partials, levels, weight)


def per_device(
    context,
    wq_cross,
    wk_cross,
    wv_cross,
    wo_cross,
    wq_latent,
    wk_latent,
    wv_latent,
    wo_latent,
    cross_keep,
    latent_keep,
    residual_keep,
):
    seq_count = lax.axis_size("seq")
    seq_index = lax.axis_index("seq")
    head_index = lax.axis_index("head")
    model_width = context.shape[1]
    head_local = cross_keep.shape[0]
    latent_count = cross_keep.shape[1]
    head_dim = wq_cross.shape[1] // head_local
    columns = model_width // lax.axis_size("head")
    local_rows = latent_count // seq_count
    first_row = seq_index * local_rows

    def project(rows, weight):
        return jnp.dot(rows, weight, preferred_element_type=jnp.float32).astype(jnp.bfloat16)

    normed = rms_rows(context)
    own_queries = project(normed[context.shape[0] - latent_count :], wq_cross)
    queries = spread(own_queries, "seq", 1)
    own_columns = lax.dynamic_slice_in_dim(
        context[context.shape[0] - latent_count :], head_index * columns, columns, 1
    )
    own_columns = jnp.where(seq_index == seq_count - 1, own_columns, 0).astype(jnp.bfloat16)
    own_columns, queries = lax.optimization_barrier((own_columns, queries))
    inputs = lax.psum_scatter(own_columns, "seq", scatter_dimension=0, tiled=True)
    key_rows = project(normed, wk_cross)
    value_rows = project(normed, wv_cross)
    partial, stats = cross_attention(
        queries, key_rows, value_rows, cross_keep, seq_count, head_dim
    )
    packed_stats = stats[:, :8].reshape(seq_count, local_rows, 8).transpose(0, 2, 1)
    partials, levels = exchange(
        [partial.reshape(seq_count, local_rows, head_local * head_dim), packed_stats],
        ["lead", "lead"],
        "seq",
        2,
    )
    levels = levels.reshape(seq_count * 8, local_rows).T
    own_branch = combine(partials, levels, wo_cross, head_local, head_dim)
    branches = exchange([own_branch], ["cols"], "head", 3)[0]
    words = lax.dynamic_slice_in_dim(residual_keep, first_row, local_rows, 1)
    blocks = columns // words.shape[2]
    flags = jnp.concatenate(
        [jnp.right_shift(words, head_index * blocks + b) & 1 for b in range(blocks)], axis=2
    ).astype(jnp.float32)
    branch = jnp.sum(branches.astype(jnp.float32), axis=0)
    latents = (inputs.astype(jnp.float32) + flags[0] * keep_scale * branch).astype(jnp.bfloat16)
    normed_latents = rms_rows(exchange([latents], ["beside"], "head", 4)[0])
    latent_queries = project(normed_latents, wq_latent)
    latent_keys = project(normed_latents, wk_latent)
    latent_values = project(normed_latents, wv_latent)
    dealt_queries, dealt_keys, dealt_values = deal(
        latent_queries, latent_keys, latent_values, "seq", head_dim, 5
    )
    group = seq_count // head_local
    places = jnp.stack(
        [seq_index // group]
        + [piece_of(t, lax.rem(seq_index, group), group) for t in range(head_local)]
    ).astype(jnp.int32)
    dealt_out = latent_attention(places, dealt_queries, dealt_keys, dealt_values, latent_keep)
    latent_attended = collect(dealt_out, "seq", 7)
    latent_branches = exchange([project(latent_attended, wo_latent)], ["cols"], "head", 6)[0]
    latent_branch = jnp.sum(latent_branches.astype(jnp.float32), axis=0)
    return (latents.astype(jnp.float32) + flags[1] * keep_scale * latent_branch).astype(
        jnp.bfloat16
    )


def solution(mesh):
    in_specs = (
        P("seq", None),
        P(None, "head"),
        P(None, "head"),
        P(None, "head"),
        P("head", None),
        P(None, "head"),
        P(None, "head"),
        P(None, "head"),
        P("head", None),
        P("head", None, "seq"),
        P("head", None, None),
        P(),
    )
    out_specs = P("seq", "head")
    return jax.shard_map(
        per_device, mesh=mesh, in_specs=in_specs, out_specs=out_specs, check_vma=False
    )
```

```python
import functools
import math

import jax
import jax.numpy as jnp
from jax import lax
from jax.experimental import pallas as pl
from jax.experimental.pallas import tpu as pltpu
from jax.sharding import PartitionSpec as P

keep_scale = 8.0 / 7.0
masked = -1e30
log2e = 1.4426950408889634
MESH = pl.DeviceIdType.MESH
ANY = pl.BlockSpec(memory_space=pl.ANY)


def rms_rows(matrix):
    wide_rows = matrix.astype(jnp.float32)
    mean_square = jnp.mean(wide_rows * wide_rows, axis=-1, keepdims=True)
    return (wide_rows * lax.rsqrt(mean_square + 1e-06)).astype(jnp.bfloat16)


def greet(axis, n, me):
    barrier = pltpu.get_barrier_semaphore()
    for d in range(1, n):
        pl.semaphore_signal(
            barrier, inc=1, device_id={axis: lax.rem(me + d, n)}, device_id_type=MESH
        )
    pl.semaphore_wait(barrier, n - 1)


def relay(src, buffer, dst, sem):
    inward = pltpu.make_async_copy(src, buffer, sem)
    inward.start()
    inward.wait()
    outward = pltpu.make_async_copy(buffer, dst, sem)
    outward.start()
    return outward


def exchange_kernel(axis, n, modes, widths, *refs):
    count = len(modes)
    ins, outs = refs[:count], refs[count : 2 * count]
    send_sem, recv_sem, local_sem = refs[2 * count : 2 * count + 3]
    buffers = refs[2 * count + 3 :]
    me = lax.axis_index(axis)

    def piece(a, j):
        if modes[a] == "lead":
            return ins[a].at[j]
        if modes[a] == "cols":
            start = pl.multiple_of(j * widths[a], 128)
            return ins[a].at[:, pl.ds(start, widths[a])]
        return ins[a]

    def place(a):
        if modes[a] == "beside":
            return outs[a].at[:, pl.ds(pl.multiple_of(me * widths[a], 128), widths[a])]
        return outs[a].at[me]

    greet(axis, n, me)
    copies = []
    for d in range(1, n):
        to = lax.rem(me + d, n)
        for a in range(count):
            copy = pltpu.make_async_remote_copy(
                src_ref=piece(a, to),
                dst_ref=place(a),
                send_sem=send_sem.at[a, d],
                recv_sem=recv_sem.at[a, d],
                device_id={axis: to},
                device_id_type=MESH,
            )
            copy.start()
            copies.append(copy)
    for a in range(count):
        copies.append(relay(piece(a, me), buffers[a], place(a), local_sem.at[a]))
    for copy in copies:
        copy.wait()


def exchange(arrays, modes, axis, ident):
    n = lax.axis_size(axis)
    shapes, widths, buffers = [], [], []
    for x, mode in zip(arrays, modes):
        if mode == "lead":
            shape, width = x.shape, 0
            own = x.shape[1:]
        elif mode == "cols":
            width = x.shape[1] // n
            shape = (n, x.shape[0], width)
            own = shape[1:]
        else:
            shape, width = (x.shape[0], n * x.shape[1]), x.shape[1]
            own = x.shape
        shapes.append(jax.ShapeDtypeStruct(shape, x.dtype))
        widths.append(width)
        buffers.append(pltpu.VMEM(own, x.dtype))
    return pl.pallas_call(
        functools.partial(exchange_kernel, axis, n, tuple(modes), tuple(widths)),
        out_shape=tuple(shapes),
        in_specs=[ANY] * len(arrays),
        out_specs=tuple([ANY] * len(arrays)),
        scratch_shapes=[
            pltpu.SemaphoreType.DMA((len(arrays), n)),
            pltpu.SemaphoreType.DMA((len(arrays), n)),
            pltpu.SemaphoreType.DMA((len(arrays),)),
        ]
        + buffers,
        compiler_params=pltpu.CompilerParams(collective_id=ident, has_side_effects=True),
    )(*arrays)


def spread_kernel(axis, n, x_ref, out_ref, send_a, recv_a, send_b, recv_b):
    me = lax.axis_index(axis)
    root = n - 1
    greet(axis, n, me)

    def parts(j):
        return (pl.ds(j * n, n), pl.ds(root * n + j, 1))

    tail = pl.ds(root * n + root, 1)

    def remote(src, dst, send, recv, to):
        return pltpu.make_async_remote_copy(
            src_ref=src,
            dst_ref=dst,
            send_sem=send,
            recv_sem=recv,
            device_id={axis: to},
            device_id_type=MESH,
        )

    @pl.when(me == root)
    def _():
        copies = []
        for j in range(root):
            for p, part in enumerate(parts(j)):
                copies.append(
                    remote(out_ref.at[part], out_ref.at[part], send_a.at[p, j], recv_a.at[p], j)
                )
                copies[-1].start()
        for j in range(root):
            copies.append(
                remote(out_ref.at[tail], out_ref.at[tail], send_a.at[2, j], recv_a.at[2], j)
            )
            copies[-1].start()
        for copy in copies:
            copy.wait_send()

    @pl.when(me != root)
    def _():
        copies = []
        for p, part in enumerate(parts(me)):
            remote(out_ref.at[part], out_ref.at[part], send_a.at[p, 0], recv_a.at[p], root).wait_recv()
            for d in range(1, root):
                to = lax.rem(me + d, root)
                copies.append(
                    remote(
                        out_ref.at[part], out_ref.at[part], send_b.at[p, d], recv_b.at[p, d], to
                    )
                )
                copies[-1].start()
        remote(out_ref.at[tail], out_ref.at[tail], send_a.at[2, 0], recv_a.at[2], root).wait_recv()
        for copy in copies:
            copy.wait()


def spread(x, axis, ident):
    n = lax.axis_size(axis)
    rows, width = x.shape
    grains = x.reshape(n * n, rows // (n * n), width)
    out = pl.pallas_call(
        functools.partial(spread_kernel, axis, n),
        out_shape=jax.ShapeDtypeStruct(grains.shape, x.dtype),
        in_specs=[ANY],
        out_specs=ANY,
        input_output_aliases={0: 0},
        scratch_shapes=[
            pltpu.SemaphoreType.DMA((3, n)),
            pltpu.SemaphoreType.DMA((3,)),
            pltpu.SemaphoreType.DMA((2, n)),
            pltpu.SemaphoreType.DMA((2, n)),
        ],
        compiler_params=pltpu.CompilerParams(collective_id=ident, has_side_effects=True),
    )(grains)
    return out.reshape(rows, width)


def piece_of(slot, sub, g):
    return slot * g + (sub if slot % 2 == 0 else g - 1 - sub)


def owner_of(me, g):
    slot, place = me // g, lax.rem(me, g)
    return slot, jnp.where(lax.rem(slot, 2) == 0, place, g - 1 - place)


def deal_kernel(axis, n, heads, hd, *refs):
    q_ref, k_ref, v_ref, qo, ko, vo, send, recv, qsend, qrecv, local, buffer = refs
    me = lax.axis_index(axis)
    g = n // heads

    def cut(ref, j):
        return ref.at[:, pl.ds(pl.multiple_of((j // g) * hd, 128), hd)]

    slot, sub = owner_of(me, g)

    def query(h):
        to = h * g + sub
        return to, pltpu.make_async_remote_copy(
            src_ref=q_ref.at[:, h * hd : (h + 1) * hd],
            dst_ref=qo.at[slot],
            send_sem=qsend.at[h],
            recv_sem=qrecv.at[slot],
            device_id={axis: to},
            device_id_type=MESH,
        )

    greet(axis, n, me)
    copies = []
    for d in range(1, n):
        to = lax.rem(me + d, n)
        for a, (ref, out) in enumerate(((k_ref, ko), (v_ref, vo))):
            copies.append(
                pltpu.make_async_remote_copy(
                    src_ref=cut(ref, to),
                    dst_ref=out.at[me],
                    send_sem=send.at[a, d],
                    recv_sem=recv.at[a, d],
                    device_id={axis: to},
                    device_id_type=MESH,
                )
            )
            copies[-1].start()
    for h in range(heads):
        to, copy = query(h)

        @pl.when(to != me)
        def _():
            copy.start()

        @pl.when(to == me)
        def _():
            relay(
                q_ref.at[:, h * hd : (h + 1) * hd], buffer.at[2], qo.at[slot], local.at[2]
            ).wait()

    copies.append(relay(cut(k_ref, me), buffer.at[0], ko.at[me], local.at[0]))
    copies.append(relay(cut(v_ref, me), buffer.at[1], vo.at[me], local.at[1]))
    for copy in copies:
        copy.wait()
    for h in range(heads):
        to, copy = query(h)

        @pl.when(to != me)
        def _():
            copy.wait_send()

    for t in range(heads):
        source = piece_of(t, lax.rem(me, g), g)

        @pl.when(source != me)
        def _():
            pltpu.make_async_remote_copy(
                src_ref=qo.at[t],
                dst_ref=qo.at[t],
                send_sem=qsend.at[t],
                recv_sem=qrecv.at[t],
                device_id={axis: source},
                device_id_type=MESH,
            ).wait_recv()


def deal(queries, keys, values, axis, hd, ident):
    n = lax.axis_size(axis)
    rows, width = queries.shape
    heads = width // hd
    whole = jax.ShapeDtypeStruct((n, rows, hd), keys.dtype)
    return pl.pallas_call(
        functools.partial(deal_kernel, axis, n, heads, hd),
        out_shape=(jax.ShapeDtypeStruct((heads, rows, hd), queries.dtype), whole, whole),
        in_specs=[ANY] * 3,
        out_specs=(ANY,) * 3,
        scratch_shapes=[
            pltpu.SemaphoreType.DMA((2, n)),
            pltpu.SemaphoreType.DMA((2, n)),
            pltpu.SemaphoreType.DMA((heads,)),
            pltpu.SemaphoreType.DMA((heads,)),
            pltpu.SemaphoreType.DMA((3,)),
            pltpu.VMEM((3, rows, hd), keys.dtype),
        ],
        compiler_params=pltpu.CompilerParams(collective_id=ident, has_side_effects=True),
    )(queries, keys, values)


def collect_kernel(axis, n, heads, hd, x_ref, out_ref, send, recv, local, buffer):
    me = lax.axis_index(axis)
    g = n // heads
    head = me // g
    cols = pl.ds(pl.multiple_of(head * hd, 128), hd)
    greet(axis, n, me)

    def outgoing(t):
        to = piece_of(t, lax.rem(me, g), g)
        return to, pltpu.make_async_remote_copy(
            src_ref=x_ref.at[t],
            dst_ref=out_ref.at[:, cols],
            send_sem=send.at[t],
            recv_sem=recv.at[head],
            device_id={axis: to},
            device_id_type=MESH,
        )

    for t in range(heads):
        to, copy = outgoing(t)

        @pl.when(to != me)
        def _():
            copy.start()

        @pl.when(to == me)
        def _():
            relay(x_ref.at[t], buffer, out_ref.at[:, cols], local).wait()

    for t in range(heads):
        to, copy = outgoing(t)

        @pl.when(to != me)
        def _():
            copy.wait_send()

    slot, sub = owner_of(me, g)
    for h in range(heads):
        source = h * g + sub

        @pl.when(source != me)
        def _():
            pltpu.make_async_remote_copy(
                src_ref=x_ref.at[0],
                dst_ref=out_ref.at[:, h * hd : (h + 1) * hd],
                send_sem=send.at[0],
                recv_sem=recv.at[h],
                device_id={axis: source},
                device_id_type=MESH,
            ).wait_recv()


def collect(x, axis, ident):
    n = lax.axis_size(axis)
    heads, rows, hd = x.shape
    return pl.pallas_call(
        functools.partial(collect_kernel, axis, n, heads, hd),
        out_shape=jax.ShapeDtypeStruct((rows, heads * hd), x.dtype),
        in_specs=[ANY],
        out_specs=ANY,
        scratch_shapes=[
            pltpu.SemaphoreType.DMA((heads,)),
            pltpu.SemaphoreType.DMA((heads,)),
            pltpu.SemaphoreType.DMA,
            pltpu.VMEM((rows, hd), x.dtype),
        ],
        compiler_params=pltpu.CompilerParams(collective_id=ident, has_side_effects=True),
    )(x)


def dot_t(a, b):
    return lax.dot_general(a, b, (((1,), (1,)), ((), ())), preferred_element_type=jnp.float32)


def fold_lanes(x, op):
    parts = [x[:, j : j + 128] for j in range(0, x.shape[1], 128)]
    return functools.reduce(op, parts)


def cross_kernel(n, hd, scale, q_ref, k_ref, v_ref, w_ref, o_ref, st_ref, s_ref):
    block, head = pl.program_id(0), pl.program_id(1)
    bq = q_ref.shape[0]
    keys = k_ref.shape[0]
    chunk = w_ref.shape[2]
    chunks = keys // chunk
    root = lax.axis_index("seq") == n - 1
    cols = pl.ds(pl.multiple_of(head * hd, 128), hd)
    factor = scale * log2e

    def finish(acc, top, total):
        o_ref[...] = (acc * (keep_scale / total)).astype(o_ref.dtype)
        stat = top * scale + jnp.log(total)
        lane = lax.broadcasted_iota(jnp.int32, st_ref.shape, 1)
        st_ref[...] = jnp.where(lane == head, stat, st_ref[...])

    @pl.when(head == 0)
    def _():
        st_ref[...] = jnp.zeros_like(st_ref)

    @pl.when(jnp.logical_not(root))
    def _():
        q = q_ref[...]
        tops = None
        for c in range(chunks):
            s = dot_t(q, k_ref[c * chunk : (c + 1) * chunk, cols])
            s_ref[c] = s
            t = fold_lanes(s, jnp.maximum)
            tops = t if tops is None else jnp.maximum(tops, t)
        top = jnp.max(tops, axis=1, keepdims=True)
        words = w_ref[0]
        acc = jnp.zeros((bq, hd), jnp.float32)
        sums = jnp.zeros((bq, 128), jnp.float32)
        for c in range(chunks):
            e = jnp.exp2((s_ref[c] - top) * factor)
            sums = sums + fold_lanes(e, jnp.add)
            weights = jnp.where((words & (1 << c)) != 0, e, 0.0).astype(jnp.bfloat16)
            acc = acc + jnp.dot(
                weights,
                v_ref[c * chunk : (c + 1) * chunk, cols],
                preferred_element_type=jnp.float32,
            )
        finish(acc, top, jnp.sum(sums, axis=1, keepdims=True))

    @pl.when(root)
    def _():
        q = q_ref[...]
        used = jnp.minimum(((block + 1) * bq + chunk - 1) // chunk, chunks)
        row = block * bq + lax.broadcasted_iota(jnp.int32, (bq, chunk), 0)
        lane = lax.broadcasted_iota(jnp.int32, (bq, chunk), 1)

        def first(c, tops):
            at = pl.ds(pl.multiple_of(c * chunk, chunk), chunk)
            s = dot_t(q, k_ref[at, cols])
            s = jnp.where(lane + c * chunk <= row, s, masked)
            s_ref[c] = s
            return jnp.maximum(tops, fold_lanes(s, jnp.maximum))

        tops = lax.fori_loop(0, used, first, jnp.full((bq, 128), masked, jnp.float32))
        top = jnp.max(tops, axis=1, keepdims=True)
        words = w_ref[0]

        def second(c, carry):
            acc, sums = carry
            at = pl.ds(pl.multiple_of(c * chunk, chunk), chunk)
            e = jnp.exp2((s_ref[c] - top) * factor)
            e = jnp.where(lane + c * chunk <= row, e, 0.0)
            sums = sums + fold_lanes(e, jnp.add)
            weights = jnp.where((words & (1 << c)) != 0, e, 0.0).astype(jnp.bfloat16)
            acc = acc + jnp.dot(weights, v_ref[at, cols], preferred_element_type=jnp.float32)
            return acc, sums

        acc, sums = lax.fori_loop(
            0,
            used,
            second,
            (jnp.zeros((bq, hd), jnp.float32), jnp.zeros((bq, 128), jnp.float32)),
        )
        finish(acc, top, jnp.sum(sums, axis=1, keepdims=True))


def cross_attention(queries, keys, values, words, n, hd):
    rows, width = queries.shape
    toks = keys.shape[0]
    heads = width // hd
    bq = min(256, rows)
    chunk = words.shape[2]
    return pl.pallas_call(
        functools.partial(cross_kernel, n, hd, 1.0 / math.sqrt(hd)),
        grid=(rows // bq, heads),
        in_specs=[
            pl.BlockSpec((bq, hd), lambda i, h: (i, h)),
            pl.BlockSpec((toks, width), lambda i, h: (0, 0)),
            pl.BlockSpec((toks, width), lambda i, h: (0, 0)),
            pl.BlockSpec((1, bq, chunk), lambda i, h: (h, i, 0)),
        ],
        out_specs=(
            pl.BlockSpec((bq, hd), lambda i, h: (i, h)),
            pl.BlockSpec((bq, 128), lambda i, h: (i, 0)),
        ),
        out_shape=(
            jax.ShapeDtypeStruct((rows, width), jnp.bfloat16),
            jax.ShapeDtypeStruct((rows, 128), jnp.float32),
        ),
        scratch_shapes=[pltpu.VMEM((toks // chunk, bq, chunk), jnp.float32)],
        cost_estimate=pl.CostEstimate(
            flops=4 * rows * toks * width * 4,
            transcendentals=heads * rows * toks,
            bytes_accessed=4 * heads * rows * chunk,
        ),
    )(queries, keys, values, words)


def latent_kernel(hd, scale, at_ref, q_ref, k_ref, v_ref, w_ref, o_ref, s_ref):
    rows = q_ref.shape[1]
    pieces, piece_rows = k_ref.shape[0], k_ref.shape[1]
    chunk = w_ref.shape[2]
    factor = scale * log2e
    row = at_ref[1 + pl.program_id(0)] * rows + lax.broadcasted_iota(jnp.int32, (rows, chunk), 0)
    lane = lax.broadcasted_iota(jnp.int32, (rows, chunk), 1)
    per = piece_rows // chunk
    q = q_ref[0]
    words = w_ref[0]
    tops = jnp.full((rows, 128), masked, jnp.float32)
    for p in range(pieces):
        s = dot_t(q, k_ref[p])
        for j in range(per):
            c = p * per + j
            part = jnp.where(lane + c * chunk <= row, s[:, j * chunk : (j + 1) * chunk], masked)
            s_ref[c] = part
            tops = jnp.maximum(tops, part)
    top = jnp.max(tops, axis=1, keepdims=True)
    acc = jnp.zeros((rows, hd), jnp.float32)
    sums = jnp.zeros((rows, 128), jnp.float32)
    for p in range(pieces):
        kept = []
        for j in range(per):
            c = p * per + j
            e = jnp.exp2((s_ref[c] - top) * factor)
            e = jnp.where(lane + c * chunk <= row, e, 0.0)
            sums = sums + e
            kept.append(jnp.where((words & (1 << c)) != 0, e, 0.0).astype(jnp.bfloat16))
        weights = jnp.concatenate(kept, axis=1) if per > 1 else kept[0]
        acc = acc + jnp.dot(weights, v_ref[p], preferred_element_type=jnp.float32)
    total = jnp.sum(sums, axis=1, keepdims=True)
    o_ref[0] = (acc * (keep_scale / total)).astype(o_ref.dtype)


def latent_attention(places, queries, keys, values, words):
    slots, rows, hd = queries.shape
    pieces, piece_rows, _ = keys.shape
    chunk = words.shape[2]
    return pl.pallas_call(
        functools.partial(latent_kernel, hd, 1.0 / math.sqrt(hd)),
        grid_spec=pltpu.PrefetchScalarGridSpec(
            num_scalar_prefetch=1,
            grid=(slots,),
            in_specs=[
                pl.BlockSpec((1, rows, hd), lambda t, at: (t, 0, 0)),
                pl.BlockSpec((pieces, piece_rows, hd), lambda t, at: (0, 0, 0)),
                pl.BlockSpec((pieces, piece_rows, hd), lambda t, at: (0, 0, 0)),
                pl.BlockSpec((1, rows, chunk), lambda t, at: (at[0], at[1 + t], 0)),
            ],
            out_specs=pl.BlockSpec((1, rows, hd), lambda t, at: (t, 0, 0)),
            scratch_shapes=[
                pltpu.VMEM((pieces * piece_rows // chunk, rows, chunk), jnp.float32)
            ],
        ),
        out_shape=jax.ShapeDtypeStruct(queries.shape, jnp.bfloat16),
    )(places, queries, keys, values, words)


def combine_kernel(n, heads, hd, stride, p_ref, level_ref, w_ref, o_ref):
    levels = level_ref[...]
    parts = []
    for h in range(heads):
        mine = [levels[:, s * stride + h : s * stride + h + 1] for s in range(n)]
        top = functools.reduce(jnp.maximum, mine)
        shares = [jnp.exp(level - top) for level in mine]
        total = functools.reduce(jnp.add, shares)
        acc = None
        for s in range(n):
            term = p_ref[s, :, h * hd : (h + 1) * hd].astype(jnp.float32) * shares[s]
            acc = term if acc is None else acc + term
        parts.append((acc / total).astype(jnp.bfloat16))
    attended = jnp.concatenate(parts, axis=1)
    o_ref[...] = jnp.dot(attended, w_ref[...], preferred_element_type=jnp.float32).astype(
        jnp.bfloat16
    )


def combine(partials, levels, weight, heads, hd):
    n, rows, _ = partials.shape
    stride = levels.shape[1] // n
    return pl.pallas_call(
        functools.partial(combine_kernel, n, heads, hd, stride),
        out_shape=jax.ShapeDtypeStruct((rows, weight.shape[1]), jnp.bfloat16),
    )(partials, levels, weight)


def per_device(
    context,
    wq_cross,
    wk_cross,
    wv_cross,
    wo_cross,
    wq_latent,
    wk_latent,
    wv_latent,
    wo_latent,
    cross_keep,
    latent_keep,
    residual_keep,
):
    seq_count = lax.axis_size("seq")
    seq_index = lax.axis_index("seq")
    head_index = lax.axis_index("head")
    model_width = context.shape[1]
    head_local = cross_keep.shape[0]
    latent_count = cross_keep.shape[1]
    head_dim = wq_cross.shape[1] // head_local
    columns = model_width // lax.axis_size("head")
    local_rows = latent_count // seq_count
    first_row = seq_index * local_rows

    def project(rows, weight):
        return jnp.dot(rows, weight, preferred_element_type=jnp.float32).astype(jnp.bfloat16)

    normed = rms_rows(context)
    own_queries = project(normed[context.shape[0] - latent_count :], wq_cross)
    queries = spread(own_queries, "seq", 1)
    own_columns = lax.dynamic_slice_in_dim(
        context[context.shape[0] - latent_count :], head_index * columns, columns, 1
    )
    own_columns = jnp.where(seq_index == seq_count - 1, own_columns, 0).astype(jnp.bfloat16)
    own_columns, queries = lax.optimization_barrier((own_columns, queries))
    inputs = lax.psum_scatter(own_columns, "seq", scatter_dimension=0, tiled=True)
    key_rows = project(normed, wk_cross)
    value_rows = project(normed, wv_cross)
    partial, stats = cross_attention(
        queries, key_rows, value_rows, cross_keep, seq_count, head_dim
    )
    packed_stats = stats[:, :8].reshape(seq_count, local_rows, 8).transpose(0, 2, 1)
    partials, levels = exchange(
        [partial.reshape(seq_count, local_rows, head_local * head_dim), packed_stats],
        ["lead", "lead"],
        "seq",
        2,
    )
    levels = levels.reshape(seq_count * 8, local_rows).T
    own_branch = combine(partials, levels, wo_cross, head_local, head_dim)
    branches = exchange([own_branch], ["cols"], "head", 3)[0]
    words = lax.dynamic_slice_in_dim(residual_keep, first_row, local_rows, 1)
    blocks = columns // words.shape[2]
    flags = jnp.concatenate(
        [jnp.right_shift(words, head_index * blocks + b) & 1 for b in range(blocks)], axis=2
    ).astype(jnp.float32)
    branch = jnp.sum(branches.astype(jnp.float32), axis=0)
    latents = (inputs.astype(jnp.float32) + flags[0] * keep_scale * branch).astype(jnp.bfloat16)
    normed_latents = rms_rows(exchange([latents], ["beside"], "head", 4)[0])
    latent_queries = project(normed_latents, wq_latent)
    latent_keys = project(normed_latents, wk_latent)
    latent_values = project(normed_latents, wv_latent)
    dealt_queries, dealt_keys, dealt_values = deal(
        latent_queries, latent_keys, latent_values, "seq", head_dim, 5
    )
    group = seq_count // head_local
    places = jnp.stack(
        [seq_index // group]
        + [piece_of(t, lax.rem(seq_index, group), group) for t in range(head_local)]
    ).astype(jnp.int32)
    dealt_out = latent_attention(places, dealt_queries, dealt_keys, dealt_values, latent_keep)
    latent_attended = collect(dealt_out, "seq", 7)
    latent_branches = exchange([project(latent_attended, wo_latent)], ["cols"], "head", 6)[0]
    latent_branch = jnp.sum(latent_branches.astype(jnp.float32), axis=0)
    return (latents.astype(jnp.float32) + flags[1] * keep_scale * latent_branch).astype(
        jnp.bfloat16
    )


def solution(mesh):
    in_specs = (
        P("seq", None),
        P(None, "head"),
        P(None, "head"),
        P(None, "head"),
        P("head", None),
        P(None, "head"),
        P(None, "head"),
        P(None, "head"),
        P("head", None),
        P("head", None, "seq"),
        P("head", None, None),
        P(),
    )
    out_specs = P("seq", "head")
    return jax.shard_map(
        per_device, mesh=mesh, in_specs=in_specs, out_specs=out_specs, check_vma=False
    )
```
